512 devices in a mesh: slab: 16 (over z, core), sub: 32 (over y, x).
Axes of the slice: x: 4, y: 8, z: 8, core: 2. Of those that a mesh axis runs over, the one named last changes fastest.
Arguments:
- velocity_field: float32 [3, 256, 1024, 512], P(None, 'slab', 'sub'), may hold values from -6 to 6
- particle_state: float32 [16384, 6, 256], P(('slab', 'sub')), as said below
- stokes_time: float32 [16384, 256], P(('slab', 'sub')), may hold values from 0.2 to 2
- box_base: int32 [16384, 3], P(('slab', 'sub')), may hold values from -2 to 511, as said below
- live_bins: int32 [512], P(('slab', 'sub')), may hold values from 1 to 32, as said below
Outputs:
- state_out: float32 [16384, 6, 256], P(('slab', 'sub'))
The draws below stay inside these ranges and needn't reach their ends.
Inputs may be any that keep to these rules, and one draw needn't show every extreme that they name: `box_base`: columns 0 and 1 lie from -2 to 14 and from -2 to 30, column 2 from 0 to 511; bin 0 has column 0 at -2 and column 2 at 511. `live_bins`: some device has all 32 slots occupied. `particle_state`: positions lie in the box's central cell, 0 to 1 in each coordinate.
All inputs are finite; a program needn't handle non-finite values.
Results may differ from the reference program's by a relative error of at most 0.0003.
Values sent between devices are 32-bit elements; how exact they have to be, the bound alone decides.
A program may use at most 64 MiB of HBM per device.

```python
import math
import jax
import jax.numpy as jnp
from jax import lax

CX = 16
CY = 32
NZ = 512
BIN_DEV = 32
PART = 256
SUBSTEPS = 4
NX = 256
NY = 1024
BINS = 16384
N_SUB = 32
DEVICES = 512


def draw_particle_state(key, part):
    key_pos = jax.random.fold_in(key, 11)
    key_vel = jax.random.fold_in(key, 12)
    position = jax.random.uniform(key_pos, (BINS, 3, PART), jnp.float32, 0.0, 1.0)
    velocity = 0.5 * jax.random.normal(key_vel, (BINS, 3, PART), jnp.float32)
    return jnp.concatenate([position, velocity], axis=1).astype(jnp.float32)


def draw_box_base(key, part):
    key_x = jax.random.fold_in(key, 21)
    key_y = jax.random.fold_in(key, 22)
    key_z = jax.random.fold_in(key, 23)
    base_x = jax.random.randint(key_x, (BINS,), -2, CX - 1)
    base_y = jax.random.randint(key_y, (BINS,), -2, CY - 1)
    base_z = jax.random.randint(key_z, (BINS,), 0, NZ)
    bases = jnp.stack([base_x, base_y, base_z], axis=1).astype(jnp.int32)
    bases = bases.at[0, 0].set(-2)
    bases = bases.at[0, 2].set(NZ - 1)
    return bases


def draw_live_bins(key, part):
    key_flag = jax.random.fold_in(key, 31)
    key_high = jax.random.fold_in(key, 32)
    key_low = jax.random.fold_in(key, 33)
    key_pick = jax.random.fold_in(key, 34)
    crowded = jax.random.randint(key_flag, (DEVICES,), 0, 4) == 0
    high_count = jax.random.randint(key_high, (DEVICES,), BIN_DEV // 2, BIN_DEV + 1)
    low_count = jax.random.randint(key_low, (DEVICES,), 1, BIN_DEV // 4 + 1)
    counts = jnp.where(crowded, high_count, low_count).astype(jnp.int32)
    chosen = jax.random.randint(key_pick, (), 0, DEVICES)
    return counts.at[chosen].set(BIN_DEV)


def shard_levels(stream_key, dims, split, least, top_value):
    factor_of, own = 1.0, jax.random.fold_in(stream_key, 6)
    for axis_at, shards_of in split:
        heights = jnp.exp(jax.random.uniform(jax.random.fold_in(own, axis_at), (shards_of,), jnp.float32, least / len(split), top_value / len(split)))
        factor_of = factor_of * jnp.repeat(heights, dims[axis_at] // shards_of).reshape([-1 if axis == axis_at else 1 for axis in range(len(dims))])
    return factor_of


def gaussian(rng, dims, scale, limit, shards=(), kind=jnp.bfloat16):
    gain = shard_levels(rng, dims, shards, -0.22, 0.18) if shards else 1.0
    array = jax.random.normal(rng, dims, jnp.float32) * scale * gain
    return jnp.minimum(jnp.maximum(array, -limit), limit).astype(kind)


def setup_inputs(seed: int = 0) -> dict:
    keys = jax.random.split(jax.random.key(seed), 6)
    velocity_field = gaussian(keys[0], (3, NX, NY, NZ), 1.0, 6.0, ((1, 16), (2, 32)), jnp.float32)
    particle_state = draw_particle_state(jax.random.fold_in(keys[5], 71), 0)
    stokes_time = jnp.clip(jnp.exp(math.log(2.0) - 2.3025851 * jax.random.uniform(keys[2], (BINS, PART), jnp.float32) ** shard_levels(keys[2], (BINS, PART), ((0, 512),), -0.2, 0.2)), 0.2, 2.0)
    box_base = draw_box_base(jax.random.fold_in(keys[5], 71), 0)
    live_bins = draw_live_bins(jax.random.fold_in(keys[5], 71), 0)
    return dict(velocity_field=velocity_field, particle_state=particle_state, stokes_time=stokes_time, box_base=box_base, live_bins=live_bins)


STEP_SIZE = 0.2


def cubic_weights(offset):
    plus = offset + 1.0
    minus = offset - 1.0
    minus_two = offset - 2.0
    return jnp.stack([-offset * minus * minus_two / 6.0, plus * minus * minus_two / 2.0,
                      -plus * offset * minus_two / 2.0, plus * offset * minus / 6.0], axis=1)


def sample(boxes, position):
    along_x = cubic_weights(position[:, 0])
    along_y = cubic_weights(position[:, 1])
    along_z = cubic_weights(position[:, 2])
    weights = along_x[:, :, None, None, :] * along_y[:, None, :, None, :] * along_z[:, None, None, :, :]
    return jnp.sum(boxes[:, :, :, :, :, None] * weights[:, None], axis=(2, 3, 4))


def advance(boxes, states, stokes):
    position = states[:, :3]
    velocity = states[:, 3:]
    rate = (1.0 / stokes)[:, None, :]
    for substep in range(SUBSTEPS):
        slope = (sample(boxes, position) - velocity) * rate
        middle_pos = position + 0.5 * STEP_SIZE * velocity
        middle_vel = velocity + 0.5 * STEP_SIZE * slope
        position = position + STEP_SIZE * middle_vel
        velocity = velocity + STEP_SIZE * (sample(boxes, middle_pos) - middle_vel) * rate
    return jnp.concatenate([position, velocity], axis=1)


def reference(velocity_field, particle_state, stokes_time, box_base, live_bins):
    all_states = particle_state.reshape(DEVICES, BIN_DEV, 6, PART)
    all_stokes = stokes_time.reshape(DEVICES, BIN_DEV, PART)
    all_bases = box_base.reshape(DEVICES, BIN_DEV, 3)

    def one_device(inputs):
        device, states, stokes, bases, live_count = inputs
        slab_index = device // N_SUB
        sub_index = device % N_SUB
        offsets = jnp.arange(4, dtype=jnp.int32)
        rows_x = (slab_index * CX + bases[:, 0:1] + offsets[None, :]) % NX
        rows_y = (sub_index * CY + bases[:, 1:2] + offsets[None, :]) % NY
        rows_z = (bases[:, 2:3] + offsets[None, :]) % NZ
        boxes = velocity_field[:, rows_x[:, :, None, None], rows_y[:, None, :, None], rows_z[:, None, None, :]]
        boxes = jnp.moveaxis(boxes, 0, 1)
        moved = advance(boxes, states, stokes)
        keep = jnp.arange(BIN_DEV, dtype=jnp.int32) < live_count
        return jnp.where(keep[:, None, None], moved, states)

    devices = jnp.arange(DEVICES, dtype=jnp.int32)
    result = lax.map(one_device, (devices, all_states, all_stokes, all_bases, live_bins))
    return result.reshape(BINS, 6, PART)
```

```python
import functools

import jax
import jax.numpy as jnp
from jax import lax
from jax.experimental import pallas as pl
from jax.experimental.pallas import tpu as pltpu
from jax.sharding import PartitionSpec as P

SUBSTEPS = 4
STEP_SIZE = 0.2
WIDTH = 2
LANES = 128
TOP = 8
ROWS = 8
LINES = 48
MESH = pl.DeviceIdType.MESH

POWERS = (
    (0.0, 1.0, 0.0, 0.0),
    (-1 / 3, -1 / 2, 1.0, -1 / 6),
    (1 / 2, -1.0, 1 / 2, 0.0),
    (-1 / 6, 1 / 2, -1 / 2, 1 / 6),
)


def power_matrix(shape, power, node, same):
    out = jnp.zeros(shape, jnp.float32)
    for p in range(4):
        for n in range(4):
            if POWERS[p][n]:
                out = jnp.where((power == p) & (node == n) & same, POWERS[p][n], out)
    return out


def dot(a, b):
    return jnp.dot(a, b, precision=lax.Precision.HIGHEST, preferred_element_type=jnp.float32)


def sample(factor, position):
    x, y, z = position
    count = len(x)
    velocity = []
    for c in range(3):
        over_x = None
        for i in (3, 2, 1, 0):
            over_y = None
            for j in (3, 2, 1, 0):
                line = ((c * 4 + i) * 4 + j) * 4
                over_z = [factor(line + 3)] * count
                for k in (2, 1, 0):
                    f = factor(line + k)
                    over_z = [over_z[n] * z[n] + f for n in range(count)]
                over_y = over_z if over_y is None else [over_y[n] * y[n] + over_z[n] for n in range(count)]
            over_x = over_y if over_x is None else [over_x[n] * x[n] + over_y[n] for n in range(count)]
        velocity.append(over_x)
    return velocity


def kernel(n_slab, n_sub, field, states, stokes, bases, live, out,
           padded, parts, moved, picked, turned, factors, local_sems, part_sems, out_sems, send_sems, recv_sems):
    g, s = lax.axis_index("slab"), lax.axis_index("sub")
    _, cx, cy, nz = field.shape
    tiles = nz // LANES
    bins, _, part = states.shape

    loads = []
    for t in range(tiles):
        loads.append(
            pltpu.make_async_copy(
                field.at[:, :, :, pl.ds(t * LANES, LANES)],
                padded.at[:, pl.ds(WIDTH, cx), t, pl.ds(TOP, cy), :],
                local_sems.at[t],
            )
        )
        loads[-1].start()
    for q in range(6):
        loads.append(pltpu.make_async_copy(states.at[:, q, :], parts.at[q], part_sems.at[q]))
        loads[-1].start()

    steps = [(dx, dy) for dx in (-1, 1) for dy in (-1, 1)] + [(0, -1), (0, 1), (-1, 0), (1, 0)]

    def peer(dx, dy):
        return (lax.rem(g + dx + n_slab, n_slab), lax.rem(s + dy + n_sub, n_sub))

    barrier = pltpu.get_barrier_semaphore()
    for dx, dy in steps:
        pl.semaphore_signal(barrier, inc=1, device_id=peer(dx, dy), device_id_type=MESH)
    pl.semaphore_wait(barrier, len(steps))

    def source(d, n):
        return {-1: (0, WIDTH), 0: (0, n), 1: (n - WIDTH, WIDTH)}[d]

    def target(d, n, origin):
        return {-1: (origin + n, WIDTH), 0: (origin, n), 1: (origin - WIDTH, WIDTH)}[d]

    halo = []
    for k, (dx, dy) in enumerate(steps):
        for t in range(tiles):
            (x0, xn), (y0, yn) = source(dx, cx), source(dy, cy)
            (u0, un), (w0, wn) = target(dx, cx, WIDTH), target(dy, cy, TOP)
            copy = pltpu.make_async_remote_copy(
                src_ref=field.at[:, pl.ds(x0, xn), pl.ds(y0, yn), pl.ds(t * LANES, LANES)],
                dst_ref=padded.at[:, pl.ds(u0, un), t, pl.ds(w0, wn), :],
                send_sem=send_sems.at[k, t],
                recv_sem=recv_sems.at[k, t],
                device_id=peer(dx, dy),
                device_id_type=MESH,
            )
            copy.start()
            halo.append(copy)

    row = lax.broadcasted_iota(jnp.int32, (LINES, LINES), 0)
    col = lax.broadcasted_iota(jnp.int32, (LINES, LINES), 1)
    along_y = power_matrix((LINES, LINES), row % 4, col % 4, row // 4 == col // 4)
    along_x = power_matrix((LINES, LINES), row // 4 % 4, col // 4 % 4, (row // 16 == col // 16) & (row % 4 == col % 4))
    along_xy = dot(along_x, along_y)
    zr = lax.broadcasted_iota(jnp.int32, (LANES, LANES), 0)
    zc = lax.broadcasted_iota(jnp.int32, (LANES, LANES), 1)
    along_z = power_matrix((LANES, LANES), zc % 4, zr % 4, zr // 4 == zc // 4)

    for copy in loads:
        copy.wait()
    for copy in halo:
        copy.wait()

    lane = lax.broadcasted_iota(jnp.int32, (4, LANES), 1)
    for b in range(bins):
        x0, y0, z0 = bases[0, b] + WIDTH, bases[1, b] + TOP, bases[2, b]
        here = z0 // LANES
        after = lax.rem(here + 1, tiles)
        first = lane >= lax.rem(z0, LANES)
        for c in range(3):
            for i in range(4):
                a = padded[c, x0 + i, here, pl.ds(y0, 4), :]
                n = padded[c, x0 + i, after, pl.ds(y0, 4), :]
                picked[b, pl.ds((c * 4 + i) * 4, 4), :] = jnp.where(first, a, n)

    wide = lax.broadcasted_iota(jnp.int32, (LINES, LANES), 1)
    boxes = jnp.zeros((LINES, LANES), jnp.float32)
    for b in range(bins):
        shift = lax.rem(4 * b + LANES - lax.rem(bases[2, b], LANES), LANES)
        boxes = jnp.where(wide // 4 == b, pltpu.roll(picked[b], shift, 1), boxes)
    boxes = dot(dot(along_xy, boxes), along_z)
    turned[:, pl.ds(0, LINES)] = boxes.T

    for group in range(bins // ROWS):
        for k in range(4):
            v = turned[pl.ds(group * ROWS * 4 + k, ROWS, stride=4), :]
            for n in range(LINES):
                factors[group, n * 4 + k] = jnp.broadcast_to(v[:, n : n + 1], (ROWS, LANES))

    halves = [pl.ds(h * LANES, LANES) for h in range(part // LANES)]

    @pl.loop(0, bins // ROWS)
    def _(group):
        rows = pl.ds(pl.multiple_of(group * ROWS, ROWS), ROWS)
        start = [[parts[q, rows, h] for h in halves] for q in range(6)]
        rate = [1.0 / stokes[rows, h] for h in halves]
        keep = group * ROWS + lax.broadcasted_iota(jnp.int32, (ROWS, LANES), 0) < live[0]
        factor = lambda n: factors[group, n]
        span = range(len(halves))

        def substep(_, state):
            x, v = state[:3], state[3:]
            u = sample(factor, x)
            a = [[(u[c][h] - v[c][h]) * rate[h] for h in span] for c in range(3)]
            xm = [[x[c][h] + 0.5 * STEP_SIZE * v[c][h] for h in span] for c in range(3)]
            vm = [[v[c][h] + 0.5 * STEP_SIZE * a[c][h] for h in span] for c in range(3)]
            x = [[x[c][h] + STEP_SIZE * vm[c][h] for h in span] for c in range(3)]
            um = sample(factor, xm)
            v = [[v[c][h] + STEP_SIZE * (um[c][h] - vm[c][h]) * rate[h] for h in span] for c in range(3)]
            return x + v

        end = lax.fori_loop(0, SUBSTEPS, substep, start)
        for q in range(6):
            for h in span:
                moved[q, rows, halves[h]] = jnp.where(keep, end[q][h], start[q][h])

    stores = []
    for q in range(6):
        stores.append(pltpu.make_async_copy(moved.at[q], out.at[:, q, :], out_sems.at[q]))
        stores[-1].start()
    for copy in stores:
        copy.wait()


def body(velocity_field, particle_state, stokes_time, box_base, live_bins):
    n_slab, n_sub = lax.axis_size("slab"), lax.axis_size("sub")
    _, cx, cy, nz = velocity_field.shape
    tiles = nz // LANES
    bins, _, part = particle_state.shape
    anywhere = pl.BlockSpec(memory_space=pl.ANY)
    vmem = pl.BlockSpec(memory_space=pltpu.VMEM)
    smem = pl.BlockSpec(memory_space=pltpu.SMEM)
    return pl.pallas_call(
        functools.partial(kernel, n_slab, n_sub),
        out_shape=jax.ShapeDtypeStruct(particle_state.shape, jnp.float32),
        in_specs=[anywhere, anywhere, vmem, smem, smem],
        out_specs=anywhere,
        scratch_shapes=[
            pltpu.VMEM((3, cx + 2 * WIDTH, tiles, cy + 2 * TOP, LANES), jnp.float32),
            pltpu.VMEM((6, bins, part), jnp.float32),
            pltpu.VMEM((6, bins, part), jnp.float32),
            pltpu.VMEM((bins, LINES, LANES), jnp.float32),
            pltpu.VMEM((LANES, LANES), jnp.float32),
            pltpu.VMEM((bins // ROWS, LINES * 4, ROWS, LANES), jnp.float32),
            pltpu.SemaphoreType.DMA((tiles,)),
            pltpu.SemaphoreType.DMA((6,)),
            pltpu.SemaphoreType.DMA((6,)),
            pltpu.SemaphoreType.DMA((8, tiles)),
            pltpu.SemaphoreType.DMA((8, tiles)),
        ],
        compiler_params=pltpu.CompilerParams(collective_id=0, has_side_effects=True),
        name="particles",
    )(velocity_field, particle_state, stokes_time, box_base.T, live_bins)


def solution(mesh):
    placed = (
        P(None, "slab", "sub", None),
        P(("slab", "sub"), None, None),
        P(("slab", "sub"), None),
        P(("slab", "sub"), None),
        P(("slab", "sub")),
    )
    return jax.shard_map(
        body, mesh=mesh, in_specs=placed, out_specs=P(("slab", "sub"), None, None), check_vma=False
    )
```

```python
import functools

import jax
import jax.numpy as jnp
from jax import lax
from jax.experimental import pallas as pl
from jax.experimental.pallas import tpu as pltpu
from jax.sharding import PartitionSpec as P

SUBSTEPS = 4
STEP_SIZE = 0.2
WIDTH = 2
LANES = 128
TOP = 8
LINES = 48
HALF = 16
MESH = pl.DeviceIdType.MESH

POWERS = (
    (-1 / 16, 9 / 16, 9 / 16, -1 / 16),
    (1 / 24, -9 / 8, 9 / 8, -1 / 24),
    (1 / 4, -1 / 4, -1 / 4, 1 / 4),
    (-1 / 6, 1 / 2, -1 / 2, 1 / 6),
)


def power_matrix(shape, power, node, same):
    out = jnp.zeros(shape, jnp.float32)
    for p in range(4):
        for n in range(4):
            out = jnp.where((power == p) & (node == n) & same, POWERS[p][n], out)
    return out


def exact_dot(a, b):
    return jnp.dot(a, b, precision=lax.Precision.HIGHEST, preferred_element_type=jnp.float32)


def split(a):
    high = a.astype(jnp.bfloat16)
    return high, (a - high.astype(jnp.float32)).astype(jnp.bfloat16)


def dot(a, b):
    return jnp.dot(a, b, preferred_element_type=jnp.float32)


def sample(high_box, low_box, position):
    x, y, z = position
    y2, z2 = y * y, z * z
    along_z = [None, z, z2, z2 * z]
    along_y = [None, y, y2, y2 * y]
    terms = []
    for a in along_y:
        for b in along_z:
            terms.append(jnp.ones_like(x) if a is None and b is None else a if b is None else b if a is None else a * b)
    high, low = split(jnp.concatenate(terms, axis=0))
    slices = dot(high_box, high) + dot(low_box, high) + dot(high_box, low)
    velocity = []
    for c in range(3):
        i = [slices[(c * 4 + i) * HALF : (c * 4 + i + 1) * HALF] for i in range(4)]
        velocity.append(((i[3] * x + i[2]) * x + i[1]) * x + i[0])
    return velocity


def kernel(n_slab, n_sub, field, states, stokes, bases_in, live, out,
           padded, parts, rates, moved, picked, planes, boxes_high, boxes_low, bases,
           local_sems, part_sems, out_sem, send_sems, recv_sems):
    comm = n_slab > 1
    _, cx, cy, nz = field.shape
    tiles = nz // LANES
    _, bins, part = states.shape

    loads = []
    for t in range(tiles):
        loads.append(
            pltpu.make_async_copy(
                field.at[:, :, :, pl.ds(t * LANES, LANES)],
                padded.at[:, pl.ds(WIDTH, cx), t, pl.ds(TOP, cy), :],
                local_sems.at[t],
            )
        )
    for n, (here, there) in enumerate(((states, parts), (stokes, rates), (bases_in, bases))):
        loads.append(pltpu.make_async_copy(here, there, part_sems.at[n]))
    for copy in loads:
        copy.start()

    halo = []
    if comm:
        g, s = lax.axis_index("slab"), lax.axis_index("sub")
        steps = [(dx, dy) for dx in (-1, 1) for dy in (-1, 1)] + [(0, -1), (0, 1), (-1, 0), (1, 0)]

        def peer(dx, dy):
            return (lax.rem(g + dx + n_slab, n_slab), lax.rem(s + dy + n_sub, n_sub))

        barrier = pltpu.get_barrier_semaphore()
        for dx, dy in steps:
            pl.semaphore_signal(barrier, inc=1, device_id=peer(dx, dy), device_id_type=MESH)
        pl.semaphore_wait(barrier, len(steps))

        def source(d, n):
            return {-1: (0, WIDTH), 0: (0, n), 1: (n - WIDTH, WIDTH)}[d]

        def target(d, n, origin):
            return {-1: (origin + n, WIDTH), 0: (origin, n), 1: (origin - WIDTH, WIDTH)}[d]

        for k, (dx, dy) in enumerate(steps):
            for t in range(tiles):
                (x0, xn), (y0, yn) = source(dx, cx), source(dy, cy)
                (u0, un), (w0, wn) = target(dx, cx, WIDTH), target(dy, cy, TOP)
                copy = pltpu.make_async_remote_copy(
                    src_ref=field.at[:, pl.ds(x0, xn), pl.ds(y0, yn), pl.ds(t * LANES, LANES)],
                    dst_ref=padded.at[:, pl.ds(u0, un), t, pl.ds(w0, wn), :],
                    send_sem=send_sems.at[k, t],
                    recv_sem=recv_sems.at[k, t],
                    device_id=peer(dx, dy),
                    device_id_type=MESH,
                )
                copy.start()
                halo.append(copy)

    row = lax.broadcasted_iota(jnp.int32, (LINES, LINES), 0)
    col = lax.broadcasted_iota(jnp.int32, (LINES, LINES), 1)
    along_y = power_matrix((LINES, LINES), row % 4, col % 4, row // 4 == col // 4)
    along_x = power_matrix((LINES, LINES), row // 4 % 4, col // 4 % 4, (row // 16 == col // 16) & (row % 4 == col % 4))
    along_xy = exact_dot(along_x, along_y)
    zr = lax.broadcasted_iota(jnp.int32, (LANES, LANES), 0)
    zc = lax.broadcasted_iota(jnp.int32, (LANES, LANES), 1)
    along_z = [
        power_matrix((LANES, LANES), zc // HALF % 4, zr % 4, zr // 4 == zc % HALF + q * HALF) for q in range(bins // HALF)
    ]

    for copy in loads:
        copy.wait()
    parts[0:3] = parts[0:3] - 0.5
    rates[...] = 1.0 / rates[...]
    moved[...] = parts[...]
    for copy in halo:
        copy.wait()

    lane = lax.broadcasted_iota(jnp.int32, (4, LANES), 1)
    for b in range(bins):
        x0, y0, z0 = bases[0, b] + WIDTH, bases[1, b] + TOP, bases[2, b]
        here = z0 // LANES
        after = lax.rem(here + 1, tiles)
        first = lane >= lax.rem(z0, LANES)
        for c in range(3):
            for i in range(4):
                a = padded[c, x0 + i, here, pl.ds(y0, 4), :]
                n = padded[c, x0 + i, after, pl.ds(y0, 4), :]
                picked[b, pl.ds((c * 4 + i) * 4, 4), :] = jnp.where(first, a, n)

    wide = lax.broadcasted_iota(jnp.int32, (LINES, LANES), 1)
    boxes = jnp.zeros((LINES, LANES), jnp.float32)
    for b in range(bins):
        shift = lax.rem(4 * b + LANES - lax.rem(bases[2, b], LANES), LANES)
        boxes = jnp.where(wide // 4 == b, pltpu.roll(picked[b], shift, 1), boxes)
    boxes = exact_dot(along_xy, boxes)
    own = lax.broadcasted_iota(jnp.int32, (HALF, LANES), 0) == lax.broadcasted_iota(jnp.int32, (HALF, LANES), 1) % HALF
    low_lane = lax.broadcasted_iota(jnp.int32, (HALF, LANES), 1) < LANES // 2
    for q in range(bins // HALF):
        planes[q] = exact_dot(boxes, along_z[q])
        for line in range(12):
            for side in range(2):
                j = 2 * side
                even = jnp.broadcast_to(planes[q, pl.ds(line * 4 + j, 1), :], (HALF, LANES))
                odd = jnp.broadcast_to(planes[q, pl.ds(line * 4 + j + 1, 1), :], (HALF, LANES))
                high, low = split(jnp.where(own, jnp.where(low_lane, even, odd), 0.0))
                at = (q, pl.ds(line * HALF, HALF), pl.ds(side * LANES, LANES))
                boxes_high[at] = high
                boxes_low[at] = low

    halves = range(bins // HALF)

    def substep(_, carry):
        state = []
        for q in halves:
            rows = pl.ds(q * HALF, HALF)
            state.append(([moved[c, rows] for c in range(3)], [moved[c + 3, rows] for c in range(3)], rates[rows]))
        u = [sample(boxes_high[q], boxes_low[q], state[q][0]) for q in halves]
        mid = []
        for q in halves:
            x, v, rate = state[q]
            vm = [v[c] + (0.5 * STEP_SIZE) * (u[q][c] - v[c]) * rate for c in range(3)]
            mid.append(([x[c] + (0.5 * STEP_SIZE) * v[c] for c in range(3)], vm))
        um = [sample(boxes_high[q], boxes_low[q], mid[q][0]) for q in halves]
        for q in halves:
            rows = pl.ds(q * HALF, HALF)
            x, v, rate = state[q]
            vm = mid[q][1]
            for c in range(3):
                moved[c, rows] = x[c] + STEP_SIZE * vm[c]
                moved[c + 3, rows] = v[c] + STEP_SIZE * (um[q][c] - vm[c]) * rate
        return carry

    lax.fori_loop(0, SUBSTEPS, substep, 0)
    keep = lax.broadcasted_iota(jnp.int32, (bins, part), 0) < live[0]
    for c in range(6):
        end = jnp.where(keep, moved[c], parts[c])
        moved[c] = end + 0.5 if c < 3 else end
    store = pltpu.make_async_copy(moved, out, out_sem)
    store.start()
    store.wait()


def body(velocity_field, particle_state, stokes_time, box_base, live_bins):
    n_slab, n_sub = lax.axis_size("slab"), lax.axis_size("sub")
    _, cx, cy, nz = velocity_field.shape
    tiles = nz // LANES
    bins, _, part = particle_state.shape
    hbm = pl.BlockSpec(memory_space=pltpu.HBM)
    by_row = (1, 0, 2)
    out = pl.pallas_call(
        functools.partial(kernel, n_slab, n_sub),
        out_shape=jax.ShapeDtypeStruct((6, bins, part), jnp.float32),
        in_specs=[hbm] * 4 + [pl.BlockSpec(memory_space=pltpu.SMEM)],
        out_specs=pl.BlockSpec(memory_space=pl.ANY),
        scratch_shapes=[
            pltpu.VMEM((3, cx + 2 * WIDTH, tiles, cy + 2 * TOP, LANES), jnp.float32),
            pltpu.VMEM((6, bins, part), jnp.float32),
            pltpu.VMEM((bins, part), jnp.float32),
            pltpu.VMEM((6, bins, part), jnp.float32),
            pltpu.VMEM((bins, LINES, LANES), jnp.float32),
            pltpu.VMEM((bins // HALF, LINES, LANES), jnp.float32),
            pltpu.VMEM((bins // HALF, 12 * HALF, 2 * LANES), jnp.bfloat16),
            pltpu.VMEM((bins // HALF, 12 * HALF, 2 * LANES), jnp.bfloat16),
            pltpu.SMEM((3, bins), jnp.int32),
            pltpu.SemaphoreType.DMA((tiles,)),
            pltpu.SemaphoreType.DMA((3,)),
            pltpu.SemaphoreType.DMA,
            pltpu.SemaphoreType.DMA((8, tiles)),
            pltpu.SemaphoreType.DMA((8, tiles)),
        ],
        compiler_params=pltpu.CompilerParams(
            collective_id=0 if n_slab > 1 else None, has_side_effects=True, vmem_limit_bytes=24 << 20
        ),
        name="particles",
    )(
        *(
            pltpu.with_memory_space_constraint(a, pltpu.HBM)
            for a in (velocity_field, particle_state.transpose(by_row), stokes_time, box_base.T)
        ),
        live_bins,
    )
    return out.transpose(by_row)


def solution(mesh):
    placed = (
        P(None, "slab", "sub", None),
        P(("slab", "sub"), None, None),
        P(("slab", "sub"), None),
        P(("slab", "sub"), None),
        P(("slab", "sub")),
    )
    return jax.shard_map(
        body, mesh=mesh, in_specs=placed, out_specs=P(("slab", "sub"), None, None), check_vma=False
    )
```

```python
import functools

import jax
import jax.numpy as jnp
from jax import lax
from jax.experimental import pallas as pl
from jax.experimental.pallas import tpu as pltpu
from jax.sharding import PartitionSpec as P

SUBSTEPS = 4
STEP_SIZE = 0.2
WIDTH = 2
LANES = 128
TOP = 8
LINES = 48
HALF = 16
MESH = pl.DeviceIdType.MESH

POWERS = (
    (-1 / 16, 9 / 16, 9 / 16, -1 / 16),
    (1 / 24, -9 / 8, 9 / 8, -1 / 24),
    (1 / 4, -1 / 4, -1 / 4, 1 / 4),
    (-1 / 6, 1 / 2, -1 / 2, 1 / 6),
)


def power_matrix(shape, power, node, same):
    out = jnp.zeros(shape, jnp.float32)
    for p in range(4):
        for n in range(4):
            out = jnp.where((power == p) & (node == n) & same, POWERS[p][n], out)
    return out


def exact_dot(a, b):
    return jnp.dot(a, b, precision=lax.Precision.HIGHEST, preferred_element_type=jnp.float32)


def split(a):
    high = a.astype(jnp.bfloat16)
    return high, (a - high.astype(jnp.float32)).astype(jnp.bfloat16)


def dot(a, b):
    return jnp.dot(a, b, preferred_element_type=jnp.float32)


def sample(high_box, low_box, position):
    x, y, z = position
    y2, z2 = y * y, z * z
    along_z = [None, z, z2, z2 * z]
    along_y = [None, y, y2, y2 * y]
    terms = []
    for a in along_y:
        for b in along_z:
            terms.append(jnp.ones_like(x) if a is None and b is None else a if b is None else b if a is None else a * b)
    high, low = split(jnp.concatenate(terms, axis=0))
    slices = dot(high_box, high) + dot(low_box, high) + dot(high_box, low)
    velocity = []
    for c in range(3):
        i = [slices[(c * 4 + i) * HALF : (c * 4 + i + 1) * HALF] for i in range(4)]
        velocity.append(((i[3] * x + i[2]) * x + i[1]) * x + i[0])
    return velocity


def kernel(n_slab, n_sub, field, states, stokes, bases_in, live, out,
           padded, parts, rates, moved, picked, planes, boxes_high, boxes_low, bases,
           local_sems, part_sems, out_sem, send_sems, recv_sems, here_sem):
    _, cx, cy, nz = field.shape
    tiles = nz // LANES
    _, bins, part = states.shape
    g, s = lax.axis_index("slab"), lax.axis_index("sub")

    def at(dx, dy):
        return (lax.rem(g + dx + n_slab, n_slab), lax.rem(s + dy + n_sub, n_sub))

    left, right, down, up = at(-1, 0), at(1, 0), at(0, -1), at(0, 1)
    odd = lax.rem(g, 2) == 1
    even = jnp.logical_not(odd)

    loads = []

    def load(xs, ys):
        copies = []
        for t in range(tiles):
            n = len(loads)
            copy = pltpu.make_async_copy(
                field.at[:, xs, ys, pl.ds(t * LANES, LANES)],
                padded.at[:, shifted(xs, WIDTH), t, shifted(ys, TOP), :],
                local_sems.at[n],
            )
            copy.start()
            loads.append(copy)
            copies.append(copy)
        return copies

    def shifted(rows, by):
        return pl.ds(rows.start + by, rows.size)

    x_first, x_last, x_inner = pl.ds(0, WIDTH), pl.ds(cx - WIDTH, WIDTH), pl.ds(WIDTH, cx - 2 * WIDTH)
    last_layers = load(x_last, pl.ds(0, cy))
    first_layers = load(x_first, pl.ds(0, cy))
    y_edges = load(x_inner, pl.ds(0, TOP)) + load(x_inner, pl.ds(cy - TOP, TOP))
    rest = load(x_inner, pl.ds(TOP, cy - 2 * TOP))
    small = []
    for n, (here, there) in enumerate(((states, parts), (stokes, rates), (bases_in, bases))):
        small.append(pltpu.make_async_copy(here, there, part_sems.at[n]))
        small[-1].start()

    barrier = pltpu.get_barrier_semaphore()
    pl.semaphore_signal(barrier, inc=1, device_id=left, device_id_type=MESH)

    @pl.when(odd)
    def _():
        for dy in (-1, 1):
            pl.semaphore_signal(barrier, inc=1, device_id=at(-1, dy), device_id_type=MESH)

    @pl.when(even)
    def _():
        for dy in (-1, 1):
            pl.semaphore_signal(barrier, inc=1, device_id=at(0, dy), device_id_type=MESH)

    pl.semaphore_wait(barrier, jnp.where(odd, 1, 5))
    pl.semaphore_signal(here_sem, inc=1, device_id=right, device_id_type=MESH)

    copies = []

    def send(to, xs, ys, dx, dy):
        n = len(copies)
        copy = pltpu.make_async_remote_copy(
            src_ref=padded.at[:, xs, :, ys, :],
            dst_ref=padded.at[:, shifted(xs, -dx * cx), :, shifted(ys, -dy * cy), :],
            send_sem=send_sems.at[n],
            recv_sem=recv_sems.at[n],
            device_id=to,
            device_id_type=MESH,
        )
        copy.start()
        copies.append(copy)
        return copy

    low, high = pl.ds(TOP, WIDTH), pl.ds(TOP + cy - WIDTH, WIDTH)
    middle = pl.ds(TOP + WIDTH, cy - 2 * WIDTH)

    def send_layers(to, xs, dx):
        corners = [send(to, xs, low, dx, 0), send(to, xs, high, dx, 0)]
        send(to, xs, middle, dx, 0)
        return corners

    for copy in last_layers:
        copy.wait()
    from_left = send_layers(right, shifted(x_last, WIDTH), 1)
    for copy in first_layers + y_edges:
        copy.wait()

    @pl.when(odd)
    def _():
        pl.semaphore_wait(here_sem, 1)

    send(up, pl.ds(WIDTH, cx), high, 0, 1)
    send(down, pl.ds(WIDTH, cx), low, 0, -1)

    @pl.when(even)
    def _():
        pl.semaphore_wait(here_sem, 1)

    from_right = send_layers(left, shifted(x_first, WIDTH), -1)

    row = lax.broadcasted_iota(jnp.int32, (LINES, LINES), 0)
    col = lax.broadcasted_iota(jnp.int32, (LINES, LINES), 1)
    along_y = power_matrix((LINES, LINES), row % 4, col % 4, row // 4 == col // 4)
    along_x = power_matrix((LINES, LINES), row // 4 % 4, col // 4 % 4, (row // 16 == col // 16) & (row % 4 == col % 4))
    along_xy = exact_dot(along_x, along_y)
    zr = lax.broadcasted_iota(jnp.int32, (LANES, LANES), 0)
    zc = lax.broadcasted_iota(jnp.int32, (LANES, LANES), 1)
    along_z = [
        power_matrix((LANES, LANES), zc // HALF % 4, zr % 4, zr // 4 == zc % HALF + q * HALF) for q in range(bins // HALF)
    ]

    for copy in small:
        copy.wait()
    parts[0:3] = parts[0:3] - 0.5
    rates[...] = 1.0 / rates[...]
    moved[...] = parts[...]

    for corners, xs in ((from_right, pl.ds(WIDTH + cx, WIDTH)), (from_left, pl.ds(0, WIDTH))):
        for copy in corners:
            copy.wait_recv()
        send(down, xs, low, 0, -1)
        send(up, xs, high, 0, 1)
    for copy in rest:
        copy.wait()
    for copy in copies:
        copy.wait_send()
        if not any(copy is corner for corner in from_left + from_right):
            copy.wait_recv()

    lane = lax.broadcasted_iota(jnp.int32, (4, LANES), 1)
    for b in range(bins):
        x0, y0, z0 = bases[0, b] + WIDTH, bases[1, b] + TOP, bases[2, b]
        here = z0 // LANES
        after = lax.rem(here + 1, tiles)
        first = lane >= lax.rem(z0, LANES)
        for c in range(3):
            for i in range(4):
                a = padded[c, x0 + i, here, pl.ds(y0, 4), :]
                n = padded[c, x0 + i, after, pl.ds(y0, 4), :]
                picked[b, pl.ds((c * 4 + i) * 4, 4), :] = jnp.where(first, a, n)

    wide = lax.broadcasted_iota(jnp.int32, (LINES, LANES), 1)
    boxes = jnp.zeros((LINES, LANES), jnp.float32)
    for b in range(bins):
        shift = lax.rem(4 * b + LANES - lax.rem(bases[2, b], LANES), LANES)
        boxes = jnp.where(wide // 4 == b, pltpu.roll(picked[b], shift, 1), boxes)
    boxes = exact_dot(along_xy, boxes)
    own = lax.broadcasted_iota(jnp.int32, (HALF, LANES), 0) == lax.broadcasted_iota(jnp.int32, (HALF, LANES), 1) % HALF
    low_lane = lax.broadcasted_iota(jnp.int32, (HALF, LANES), 1) < LANES // 2
    for q in range(bins // HALF):
        planes[q] = exact_dot(boxes, along_z[q])
        for line in range(12):
            for side in range(2):
                j = 2 * side
                even = jnp.broadcast_to(planes[q, pl.ds(line * 4 + j, 1), :], (HALF, LANES))
                odd = jnp.broadcast_to(planes[q, pl.ds(line * 4 + j + 1, 1), :], (HALF, LANES))
                high, low = split(jnp.where(own, jnp.where(low_lane, even, odd), 0.0))
                at = (q, pl.ds(line * HALF, HALF), pl.ds(side * LANES, LANES))
                boxes_high[at] = high
                boxes_low[at] = low

    halves = range(bins // HALF)

    def substep(_, carry):
        state = []
        for q in halves:
            rows = pl.ds(q * HALF, HALF)
            state.append(([moved[c, rows] for c in range(3)], [moved[c + 3, rows] for c in range(3)], rates[rows]))
        u = [sample(boxes_high[q], boxes_low[q], state[q][0]) for q in halves]
        mid = []
        for q in halves:
            x, v, rate = state[q]
            vm = [v[c] + (0.5 * STEP_SIZE) * (u[q][c] - v[c]) * rate for c in range(3)]
            mid.append(([x[c] + (0.5 * STEP_SIZE) * v[c] for c in range(3)], vm))
        um = [sample(boxes_high[q], boxes_low[q], mid[q][0]) for q in halves]
        for q in halves:
            rows = pl.ds(q * HALF, HALF)
            x, v, rate = state[q]
            vm = mid[q][1]
            for c in range(3):
                moved[c, rows] = x[c] + STEP_SIZE * vm[c]
                moved[c + 3, rows] = v[c] + STEP_SIZE * (um[q][c] - vm[c]) * rate
        return carry

    lax.fori_loop(0, SUBSTEPS, substep, 0)
    keep = lax.broadcasted_iota(jnp.int32, (bins, part), 0) < live[0]
    for c in range(6):
        end = jnp.where(keep, moved[c], parts[c])
        moved[c] = end + 0.5 if c < 3 else end
    store = pltpu.make_async_copy(moved, out, out_sem)
    store.start()
    store.wait()


def body(velocity_field, particle_state, stokes_time, box_base, live_bins):
    n_slab, n_sub = lax.axis_size("slab"), lax.axis_size("sub")
    _, cx, cy, nz = velocity_field.shape
    tiles = nz // LANES
    bins, _, part = particle_state.shape
    hbm = pl.BlockSpec(memory_space=pltpu.HBM)
    by_row = (1, 0, 2)
    out = pl.pallas_call(
        functools.partial(kernel, n_slab, n_sub),
        out_shape=jax.ShapeDtypeStruct((6, bins, part), jnp.float32),
        in_specs=[hbm] * 4 + [pl.BlockSpec(memory_space=pltpu.SMEM)],
        out_specs=pl.BlockSpec(memory_space=pl.ANY),
        scratch_shapes=[
            pltpu.VMEM((3, cx + 2 * WIDTH, tiles, cy + 2 * TOP, LANES), jnp.float32),
            pltpu.VMEM((6, bins, part), jnp.float32),
            pltpu.VMEM((bins, part), jnp.float32),
            pltpu.VMEM((6, bins, part), jnp.float32),
            pltpu.VMEM((bins, LINES, LANES), jnp.float32),
            pltpu.VMEM((bins // HALF, LINES, LANES), jnp.float32),
            pltpu.VMEM((bins // HALF, 12 * HALF, 2 * LANES), jnp.bfloat16),
            pltpu.VMEM((bins // HALF, 12 * HALF, 2 * LANES), jnp.bfloat16),
            pltpu.SMEM((3, bins), jnp.int32),
            pltpu.SemaphoreType.DMA((5 * tiles,)),
            pltpu.SemaphoreType.DMA((3,)),
            pltpu.SemaphoreType.DMA,
            pltpu.SemaphoreType.DMA((12,)),
            pltpu.SemaphoreType.DMA((12,)),
            pltpu.SemaphoreType.REGULAR,
        ],
        compiler_params=pltpu.CompilerParams(
            collective_id=0, has_side_effects=True, vmem_limit_bytes=24 << 20
        ),
        name="particles",
    )(
        *(
            pltpu.with_memory_space_constraint(a, pltpu.HBM)
            for a in (velocity_field, particle_state.transpose(by_row), stokes_time, box_base.T)
        ),
        live_bins,
    )
    return out.transpose(by_row)


def solution(mesh):
    placed = (
        P(None, "slab", "sub", None),
        P(("slab", "sub"), None, None),
        P(("slab", "sub"), None),
        P(("slab", "sub"), None),
        P(("slab", "sub")),
    )
    return jax.shard_map(
        body, mesh=mesh, in_specs=placed, out_specs=P(("slab", "sub"), None, None), check_vma=False
    )
```

```python
import functools

import jax
import jax.numpy as jnp
from jax import lax
from jax.experimental import pallas as pl
from jax.experimental.pallas import tpu as pltpu
from jax.sharding import PartitionSpec as P

SUBSTEPS = 4
STEP_SIZE = 0.2
WIDTH = 2
LANES = 128
TOP = 8
LINES = 48
HALF = 16
MESH = pl.DeviceIdType.MESH

POWERS = (
    (-1 / 16, 9 / 16, 9 / 16, -1 / 16),
    (1 / 24, -9 / 8, 9 / 8, -1 / 24),
    (1 / 4, -1 / 4, -1 / 4, 1 / 4),
    (-1 / 6, 1 / 2, -1 / 2, 1 / 6),
)


def power_matrix(shape, power, node, same):
    out = jnp.zeros(shape, jnp.float32)
    for p in range(4):
        for n in range(4):
            out = jnp.where((power == p) & (node == n) & same, POWERS[p][n], out)
    return out


def exact_dot(a, b):
    return jnp.dot(a, b, precision=lax.Precision.HIGHEST, preferred_element_type=jnp.float32)


def split(a):
    high = a.astype(jnp.bfloat16)
    return high, (a - high.astype(jnp.float32)).astype(jnp.bfloat16)


def dot(a, b):
    return jnp.dot(a, b, preferred_element_type=jnp.float32)


def sample(box, position):
    x, y, z = position
    y2, z2 = y * y, z * z
    along_z = [None, z, z2, z2 * z]
    along_y = [None, y, y2, y2 * y]
    terms = []
    for a in along_y:
        for b in along_z:
            terms.append(jnp.ones_like(x) if a is None and b is None else a if b is None else b if a is None else a * b)
    high, low = split(jnp.concatenate(terms, axis=0))
    rows = 12 * HALF
    both = dot(box, high)
    slices = both[:rows] + dot(box[:rows], low) + both[rows:]
    velocity = []
    for c in range(3):
        i = [slices[(i * 3 + c) * HALF : (i * 3 + c + 1) * HALF] for i in range(4)]
        velocity.append(((i[3] * x + i[2]) * x + i[1]) * x + i[0])
    return velocity


def kernel(n_slab, n_sub, field, states, stokes, bases_in, live, out,
           padded, parts, rates, moved, picked, planes, boxes_split, bases,
           local_sems, part_sems, out_sem, send_sems, recv_sems, here_sems):
    _, cx, cy, nz = field.shape
    tiles = nz // LANES
    _, bins, part = states.shape
    g, s = lax.axis_index("slab"), lax.axis_index("sub")

    def at(dx, dy):
        return (lax.rem(g + dx + n_slab, n_slab), lax.rem(s + dy + n_sub, n_sub))

    left, right, down, up = at(-1, 0), at(1, 0), at(0, -1), at(0, 1)
    odd = lax.rem(g, 2) == 1
    even = jnp.logical_not(odd)

    loads = []

    def load(xs, ys):
        copies = []
        for t in range(tiles):
            n = len(loads)
            copy = pltpu.make_async_copy(
                field.at[:, xs, ys, pl.ds(t * LANES, LANES)],
                padded.at[:, shifted(xs, WIDTH), t, shifted(ys, TOP), :],
                local_sems.at[n],
            )
            copy.start()
            loads.append(copy)
            copies.append(copy)
        return copies

    def shifted(rows, by):
        return pl.ds(rows.start + by, rows.size)

    x_first, x_last, x_inner = pl.ds(0, WIDTH), pl.ds(cx - WIDTH, WIDTH), pl.ds(WIDTH, cx - 2 * WIDTH)
    last_layers = load(x_last, pl.ds(0, cy))
    first_layers = load(x_first, pl.ds(0, cy))
    y_edges = load(x_inner, pl.ds(0, TOP)) + load(x_inner, pl.ds(cy - TOP, TOP))
    rest = load(x_inner, pl.ds(TOP, cy - 2 * TOP))
    small = []
    for n, (here, there) in enumerate(((states, parts), (stokes, rates), (bases_in, bases))):
        small.append(pltpu.make_async_copy(here, there, part_sems.at[n]))
        small[-1].start()

    first, second, third, last = g == 0, g == 1, g == 2, g == n_slab - 1
    barrier = pltpu.get_barrier_semaphore()

    def tell(*offsets):
        for dx, dy in offsets:
            pl.semaphore_signal(barrier, inc=1, device_id=at(dx, dy), device_id_type=MESH)

    tell((-1, 0))

    @pl.when(even)
    def _():
        tell((0, -1), (0, 1))

    @pl.when(odd & jnp.logical_not(last))
    def _():
        tell((1, 0))

    @pl.when(odd & jnp.logical_not(second))
    def _():
        tell((-1, -1), (-1, 1))

    @pl.when(second)
    def _():
        tell((1, -1), (1, 1))

    pl.semaphore_wait(barrier, jnp.where(odd, 1, jnp.where(first, 3, jnp.where(third, 8, 6))))

    @pl.when(even | last)
    def _():
        pl.semaphore_signal(here_sems.at[0], inc=1, device_id=right, device_id_type=MESH)

    @pl.when(third)
    def _():
        pl.semaphore_signal(here_sems.at[1], inc=1, device_id=left, device_id_type=MESH)

    copies = []

    def remote(to, source, target):
        n = len(copies)
        copy = pltpu.make_async_remote_copy(
            src_ref=source,
            dst_ref=target,
            send_sem=send_sems.at[n],
            recv_sem=recv_sems.at[n],
            device_id=to,
            device_id_type=MESH,
        )
        copies.append(copy)
        return copy

    def cells(to, xs, ys, dx, dy):
        return remote(
            to, padded.at[:, xs, :, ys, :], padded.at[:, shifted(xs, -dx * cx), :, shifted(ys, -dy * cy), :]
        )

    low, high = pl.ds(TOP, WIDTH), pl.ds(TOP + cy - WIDTH, WIDTH)
    middle = pl.ds(TOP + WIDTH, cy - 2 * WIDTH)

    def corner_cells(to, xs, dx):
        return [
            remote(
                to,
                field.at[:, xs, ys, pl.ds(t * LANES, LANES)],
                padded.at[:, shifted(xs, WIDTH - dx * cx), t, shifted(ys, TOP), :],
            )
            for ys in (pl.ds(0, WIDTH), pl.ds(cy - WIDTH, WIDTH))
            for t in range(tiles)
        ]

    from_left, from_right = corner_cells(right, x_last, 1), corner_cells(left, x_first, -1)
    layers_left = cells(right, shifted(x_last, WIDTH), middle, 1, 0)
    layers_right = cells(left, shifted(x_first, WIDTH), middle, -1, 0)
    rows_down, rows_up = cells(up, pl.ds(WIDTH, cx), high, 0, 1), cells(down, pl.ds(WIDTH, cx), low, 0, -1)

    for copy in from_left:
        copy.start()
    for copy in last_layers:
        copy.wait()
    layers_left.start()

    later = first | second

    @pl.when(odd & jnp.logical_not(second))
    def _():
        pl.semaphore_wait(here_sems.at[0], 1)

    @pl.when(jnp.logical_not(later))
    def _():
        for copy in from_right:
            copy.start()

    for copy in first_layers:
        copy.wait()

    @pl.when(jnp.logical_not(later))
    def _():
        layers_right.start()

    for copy in y_edges:
        copy.wait()

    @pl.when(second)
    def _():
        pl.semaphore_wait(here_sems.at[1], 1)

    rows_down.start()
    rows_up.start()

    row = lax.broadcasted_iota(jnp.int32, (LINES, LINES), 0)
    col = lax.broadcasted_iota(jnp.int32, (LINES, LINES), 1)
    along_y = power_matrix((LINES, LINES), row % 4, col % 4, row // 4 == col // 4)
    along_x = power_matrix((LINES, LINES), row // 12, col // 12, row % 12 == col % 12)
    along_xy = exact_dot(along_x, along_y)
    zr = lax.broadcasted_iota(jnp.int32, (LANES, LANES), 0)
    zc = lax.broadcasted_iota(jnp.int32, (LANES, LANES), 1)
    along_z = [
        power_matrix((LANES, LANES), zc // HALF % 4, zr % 4, zr // 4 == zc % HALF + q * HALF) for q in range(bins // HALF)
    ]

    for copy in small:
        copy.wait()
    parts[0:3] = parts[0:3] - 0.5
    rates[...] = 1.0 / rates[...]
    moved[...] = parts[...]

    @pl.when(later)
    def _():
        pl.semaphore_wait(here_sems.at[0], 1)
        for copy in from_right:
            copy.start()
        layers_right.start()

    for corners, xs in ((from_right, pl.ds(WIDTH + cx, WIDTH)), (from_left, pl.ds(0, WIDTH))):
        for copy in corners:
            copy.wait_recv()
        for to, rows, dy in ((down, low, -1), (up, high, 1)):
            cells(to, xs, rows, 0, dy).start()
    for copy in rest:
        copy.wait()

    lane = lax.broadcasted_iota(jnp.int32, (4, LANES), 1)

    def pick(layers):
        for b in range(bins):
            x0, y0, z0 = bases[0, b] + WIDTH, bases[1, b] + TOP, bases[2, b]
            here = z0 // LANES
            after = lax.rem(here + 1, tiles)
            first = lane >= lax.rem(z0, LANES)
            for i in layers:
                for c in range(3):
                    a = padded[c, x0 + i, here, pl.ds(y0, 4), :]
                    n = padded[c, x0 + i, after, pl.ds(y0, 4), :]
                    picked[b, pl.ds((i * 3 + c) * 4, 4), :] = jnp.where(first, a, n)

    for copy in copies:
        copy.wait_send()
        if not any(copy is corner for corner in from_left + from_right):
            copy.wait_recv()
    pick(range(4))

    wide = lax.broadcasted_iota(jnp.int32, (LINES, LANES), 1)
    boxes = jnp.zeros((LINES, LANES), jnp.float32)
    for b in range(bins):
        shift = lax.rem(4 * b + LANES - lax.rem(bases[2, b], LANES), LANES)
        boxes = jnp.where(wide // 4 == b, pltpu.roll(picked[b], shift, 1), boxes)
    boxes = exact_dot(along_xy, boxes)
    own = lax.broadcasted_iota(jnp.int32, (HALF, LANES), 0) == lax.broadcasted_iota(jnp.int32, (HALF, LANES), 1) % HALF
    low_lane = lax.broadcasted_iota(jnp.int32, (HALF, LANES), 1) < LANES // 2
    for q in range(bins // HALF):
        planes[q] = exact_dot(boxes, along_z[q])
        for line in range(12):
            for side in range(2):
                j = 2 * side
                even = jnp.broadcast_to(planes[q, pl.ds(line * 4 + j, 1), :], (HALF, LANES))
                odd = jnp.broadcast_to(planes[q, pl.ds(line * 4 + j + 1, 1), :], (HALF, LANES))
                high, low = split(jnp.where(own, jnp.where(low_lane, even, odd), 0.0))
                lanes = pl.ds(side * LANES, LANES)
                boxes_split[q, pl.ds(line * HALF, HALF), lanes] = high
                boxes_split[q, pl.ds((line + 12) * HALF, HALF), lanes] = low

    halves = range(bins // HALF)

    def substep(_, carry):
        state = []
        for q in halves:
            rows = pl.ds(q * HALF, HALF)
            state.append(([moved[c, rows] for c in range(3)], [moved[c + 3, rows] for c in range(3)], rates[rows]))
        u = [sample(boxes_split[q], state[q][0]) for q in halves]
        mid = []
        for q in halves:
            x, v, rate = state[q]
            vm = [v[c] + (0.5 * STEP_SIZE) * (u[q][c] - v[c]) * rate for c in range(3)]
            mid.append(([x[c] + (0.5 * STEP_SIZE) * v[c] for c in range(3)], vm))
        um = [sample(boxes_split[q], mid[q][0]) for q in halves]
        for q in halves:
            rows = pl.ds(q * HALF, HALF)
            x, v, rate = state[q]
            vm = mid[q][1]
            for c in range(3):
                moved[c, rows] = x[c] + STEP_SIZE * vm[c]
                moved[c + 3, rows] = v[c] + STEP_SIZE * (um[q][c] - vm[c]) * rate
        return carry

    lax.fori_loop(0, SUBSTEPS, substep, 0)
    keep = lax.broadcasted_iota(jnp.int32, (bins, part), 0) < live[0]
    for c in range(6):
        end = jnp.where(keep, moved[c], parts[c])
        moved[c] = end + 0.5 if c < 3 else end
    store = pltpu.make_async_copy(moved, out, out_sem)
    store.start()
    store.wait()


def body(velocity_field, particle_state, stokes_time, box_base, live_bins):
    n_slab, n_sub = lax.axis_size("slab"), lax.axis_size("sub")
    _, cx, cy, nz = velocity_field.shape
    tiles = nz // LANES
    bins, _, part = particle_state.shape
    hbm = pl.BlockSpec(memory_space=pltpu.HBM)
    by_row = (1, 0, 2)
    out = pl.pallas_call(
        functools.partial(kernel, n_slab, n_sub),
        out_shape=jax.ShapeDtypeStruct((6, bins, part), jnp.float32),
        in_specs=[hbm] * 4 + [pl.BlockSpec(memory_space=pltpu.SMEM)],
        out_specs=pl.BlockSpec(memory_space=pl.ANY),
        scratch_shapes=[
            pltpu.VMEM((3, cx + 2 * WIDTH, tiles, cy + 2 * TOP, LANES), jnp.float32),
            pltpu.VMEM((6, bins, part), jnp.float32),
            pltpu.VMEM((bins, part), jnp.float32),
            pltpu.VMEM((6, bins, part), jnp.float32),
            pltpu.VMEM((bins, LINES, LANES), jnp.float32),
            pltpu.VMEM((bins // HALF, LINES, LANES), jnp.float32),
            pltpu.VMEM((bins // HALF, 24 * HALF, 2 * LANES), jnp.bfloat16),
            pltpu.SMEM((3, bins), jnp.int32),
            pltpu.SemaphoreType.DMA((5 * tiles,)),
            pltpu.SemaphoreType.DMA((3,)),
            pltpu.SemaphoreType.DMA,
            pltpu.SemaphoreType.DMA((4 * tiles + 8,)),
            pltpu.SemaphoreType.DMA((4 * tiles + 8,)),
            pltpu.SemaphoreType.REGULAR((2,)),
        ],
        compiler_params=pltpu.CompilerParams(
            collective_id=0, has_side_effects=True, vmem_limit_bytes=24 << 20
        ),
        name="particles",
    )(
        *(
            pltpu.with_memory_space_constraint(a, pltpu.HBM)
            for a in (velocity_field, particle_state.transpose(by_row), stokes_time, box_base.T)
        ),
        live_bins,
    )
    return out.transpose(by_row)


def solution(mesh):
    placed = (
        P(None, "slab", "sub", None),
        P(("slab", "sub"), None, None),
        P(("slab", "sub"), None),
        P(("slab", "sub"), None),
        P(("slab", "sub")),
    )
    return jax.shard_map(
        body, mesh=mesh, in_specs=placed, out_specs=P(("slab", "sub"), None, None), check_vma=False
    )
```

```python
import functools

import jax
import jax.numpy as jnp
from jax import lax
from jax.experimental import pallas as pl
from jax.experimental.pallas import tpu as pltpu
from jax.sharding import PartitionSpec as P

SUBSTEPS = 4
STEP_SIZE = 0.2
WIDTH = 2
LANES = 128
TOP = 8
LINES = 48
HALF = 16
MESH = pl.DeviceIdType.MESH

POWERS = (
    (-1 / 16, 9 / 16, 9 / 16, -1 / 16),
    (1 / 24, -9 / 8, 9 / 8, -1 / 24),
    (1 / 4, -1 / 4, -1 / 4, 1 / 4),
    (-1 / 6, 1 / 2, -1 / 2, 1 / 6),
)


def power_matrix(shape, power, node, same):
    out = jnp.zeros(shape, jnp.float32)
    for p in range(4):
        for n in range(4):
            out = jnp.where((power == p) & (node == n) & same, POWERS[p][n], out)
    return out


def exact_dot(a, b):
    return jnp.dot(a, b, precision=lax.Precision.HIGHEST, preferred_element_type=jnp.float32)


def split(a):
    high = a.astype(jnp.bfloat16)
    return high, (a - high.astype(jnp.float32)).astype(jnp.bfloat16)


def dot(a, b):
    return jnp.dot(a, b, preferred_element_type=jnp.float32)


def sample(box, position):
    x, y, z = position
    y2, z2 = y * y, z * z
    along_z = [None, z, z2, z2 * z]
    along_y = [None, y, y2, y2 * y]
    terms = []
    for a in along_y:
        for b in along_z:
            terms.append(jnp.ones_like(x) if a is None and b is None else a if b is None else b if a is None else a * b)
    high, low = split(jnp.concatenate(terms, axis=0))
    rows = 12 * HALF
    both = dot(box, high)
    slices = both[:rows] + dot(box[:rows], low) + both[rows:]
    velocity = []
    for c in range(3):
        i = [slices[(i * 3 + c) * HALF : (i * 3 + c + 1) * HALF] for i in range(4)]
        velocity.append(((i[3] * x + i[2]) * x + i[1]) * x + i[0])
    return velocity


def kernel(n_slab, n_sub, field, states, stokes, bases_in, live, out,
           padded, parts, rates, moved, picked, planes, boxes_split, bases,
           local_sems, part_sems, out_sem, send_sems, recv_sems, here_sems):
    _, cx, cy, nz = field.shape
    tiles = nz // LANES
    _, bins, part = states.shape
    g, s = lax.axis_index("slab"), lax.axis_index("sub")

    def at(dx, dy):
        return (lax.rem(g + dx + n_slab, n_slab), lax.rem(s + dy + n_sub, n_sub))

    left, right, down, up = at(-1, 0), at(1, 0), at(0, -1), at(0, 1)
    odd = lax.rem(g, 2) == 1
    even = jnp.logical_not(odd)

    loads = []

    def load(xs, ys):
        copies = []
        for t in range(tiles):
            n = len(loads)
            copy = pltpu.make_async_copy(
                field.at[:, xs, ys, pl.ds(t * LANES, LANES)],
                padded.at[:, shifted(xs, WIDTH), t, shifted(ys, TOP), :],
                local_sems.at[n],
            )
            copy.start()
            loads.append(copy)
            copies.append(copy)
        return copies

    def shifted(rows, by):
        return pl.ds(rows.start + by, rows.size)

    x_first, x_last, x_inner = pl.ds(0, WIDTH), pl.ds(cx - WIDTH, WIDTH), pl.ds(WIDTH, cx - 2 * WIDTH)
    last_layers = load(x_last, pl.ds(0, cy))
    y_edges = load(x_inner, pl.ds(0, TOP)) + load(x_inner, pl.ds(cy - TOP, TOP))
    first_layers = load(x_first, pl.ds(0, cy))
    rest = load(x_inner, pl.ds(TOP, cy - 2 * TOP))
    small = []
    for n, (here, there) in enumerate(((states, parts), (stokes, rates), (bases_in, bases))):
        small.append(pltpu.make_async_copy(here, there, part_sems.at[n]))
        small[-1].start()

    first, second, third, last = g == 0, g == 1, g == 2, g == n_slab - 1
    barrier = pltpu.get_barrier_semaphore()

    def tell(*offsets):
        for dx, dy in offsets:
            pl.semaphore_signal(barrier, inc=1, device_id=at(dx, dy), device_id_type=MESH)

    tell((-1, 0))

    @pl.when(even)
    def _():
        tell((0, -1), (0, 1))

    @pl.when(odd & jnp.logical_not(last))
    def _():
        tell((1, 0))

    @pl.when(odd & jnp.logical_not(second))
    def _():
        tell((-1, -1), (-1, 1))

    @pl.when(second)
    def _():
        tell((1, -1), (1, 1))

    pl.semaphore_wait(barrier, jnp.where(odd, 1, jnp.where(first, 3, jnp.where(third, 8, 6))))

    @pl.when(even | last)
    def _():
        pl.semaphore_signal(here_sems.at[0], inc=1, device_id=right, device_id_type=MESH)

    @pl.when(third)
    def _():
        pl.semaphore_signal(here_sems.at[1], inc=1, device_id=left, device_id_type=MESH)

    copies = []

    def remote(to, source, target):
        n = len(copies)
        copy = pltpu.make_async_remote_copy(
            src_ref=source,
            dst_ref=target,
            send_sem=send_sems.at[n],
            recv_sem=recv_sems.at[n],
            device_id=to,
            device_id_type=MESH,
        )
        copies.append(copy)
        return copy

    def cells(to, xs, ys, dx, dy):
        return remote(
            to, padded.at[:, xs, :, ys, :], padded.at[:, shifted(xs, -dx * cx), :, shifted(ys, -dy * cy), :]
        )

    low, high = pl.ds(TOP, WIDTH), pl.ds(TOP + cy - WIDTH, WIDTH)
    middle = pl.ds(TOP + WIDTH, cy - 2 * WIDTH)

    def corner_cells(to, xs, dx):
        return [
            remote(
                to,
                field.at[:, xs, ys, pl.ds(t * LANES, LANES)],
                padded.at[:, shifted(xs, WIDTH - dx * cx), t, shifted(ys, TOP), :],
            )
            for ys in (pl.ds(0, WIDTH), pl.ds(cy - WIDTH, WIDTH))
            for t in range(tiles)
        ]

    from_left, from_right = corner_cells(right, x_last, 1), corner_cells(left, x_first, -1)
    layers_left = cells(right, shifted(x_last, WIDTH), middle, 1, 0)
    layers_right = cells(left, shifted(x_first, WIDTH), middle, -1, 0)
    rows_down, rows_up = cells(up, pl.ds(WIDTH, cx), high, 0, 1), cells(down, pl.ds(WIDTH, cx), low, 0, -1)

    for copy in from_left:
        copy.start()
    for copy in last_layers:
        copy.wait()
    layers_left.start()

    later = first | second

    @pl.when(odd & jnp.logical_not(second))
    def _():
        pl.semaphore_wait(here_sems.at[0], 1)

    @pl.when(jnp.logical_not(later))
    def _():
        for copy in from_right:
            copy.start()

    for copy in first_layers:
        copy.wait()

    @pl.when(jnp.logical_not(later))
    def _():
        layers_right.start()

    for copy in y_edges:
        copy.wait()

    @pl.when(second)
    def _():
        pl.semaphore_wait(here_sems.at[1], 1)

    rows_down.start()
    rows_up.start()

    row = lax.broadcasted_iota(jnp.int32, (LINES, LINES), 0)
    col = lax.broadcasted_iota(jnp.int32, (LINES, LINES), 1)
    along_y = power_matrix((LINES, LINES), row % 4, col % 4, row // 4 == col // 4)
    along_x = power_matrix((LINES, LINES), row // 12, col // 12, row % 12 == col % 12)
    along_xy = exact_dot(along_x, along_y)
    zr = lax.broadcasted_iota(jnp.int32, (LANES, LANES), 0)
    zc = lax.broadcasted_iota(jnp.int32, (LANES, LANES), 1)
    along_z = [
        power_matrix((LANES, LANES), zc // HALF % 4, zr % 4, zr // 4 == zc % HALF + q * HALF) for q in range(bins // HALF)
    ]

    for copy in small:
        copy.wait()
    parts[0:3] = parts[0:3] - 0.5
    rates[...] = 1.0 / rates[...]
    moved[...] = parts[...]

    @pl.when(later)
    def _():
        pl.semaphore_wait(here_sems.at[0], 1)
        for copy in from_right:
            copy.start()
        layers_right.start()

    for corners, xs in ((from_right, pl.ds(WIDTH + cx, WIDTH)), (from_left, pl.ds(0, WIDTH))):
        for copy in corners:
            copy.wait_recv()
        for to, rows, dy in ((down, low, -1), (up, high, 1)):
            cells(to, xs, rows, 0, dy).start()
    for copy in rest:
        copy.wait()

    lane = lax.broadcasted_iota(jnp.int32, (4, LANES), 1)

    def pick(layers):
        for b in range(bins):
            x0, y0, z0 = bases[0, b] + WIDTH, bases[1, b] + TOP, bases[2, b]
            here = lax.shift_right_logical(z0, 7)
            after = (here + 1) & (tiles - 1)
            first = lane >= (z0 & (LANES - 1))
            for i in layers:
                for c in range(3):
                    a = padded[c, x0 + i, here, pl.ds(y0, 4), :]
                    n = padded[c, x0 + i, after, pl.ds(y0, 4), :]
                    picked[b, pl.ds((i * 3 + c) * 4, 4), :] = jnp.where(first, a, n)

    for copy in copies:
        copy.wait_send()
        if not any(copy is corner for corner in from_left + from_right):
            copy.wait_recv()
    pick(range(4))

    wide = lax.broadcasted_iota(jnp.int32, (LINES, LANES), 1)
    boxes = jnp.zeros((LINES, LANES), jnp.float32)
    for b in range(bins):
        shift = (4 * b - bases[2, b]) & (LANES - 1)
        boxes = jnp.where(wide // 4 == b, pltpu.roll(picked[b], shift, 1), boxes)
    boxes = exact_dot(along_xy, boxes)
    own = lax.broadcasted_iota(jnp.int32, (HALF, LANES), 0) == lax.broadcasted_iota(jnp.int32, (HALF, LANES), 1) % HALF
    low_lane = lax.broadcasted_iota(jnp.int32, (HALF, LANES), 1) < LANES // 2
    for q in range(bins // HALF):
        planes[q] = exact_dot(boxes, along_z[q])
        for line in range(12):
            for side in range(2):
                j = 2 * side
                even = jnp.broadcast_to(planes[q, pl.ds(line * 4 + j, 1), :], (HALF, LANES))
                odd = jnp.broadcast_to(planes[q, pl.ds(line * 4 + j + 1, 1), :], (HALF, LANES))
                high, low = split(jnp.where(own, jnp.where(low_lane, even, odd), 0.0))
                lanes = pl.ds(side * LANES, LANES)
                boxes_split[q, pl.ds(line * HALF, HALF), lanes] = high
                boxes_split[q, pl.ds((line + 12) * HALF, HALF), lanes] = low

    halves = range(bins // HALF)

    def substep(_, carry):
        state = []
        for q in halves:
            rows = pl.ds(q * HALF, HALF)
            state.append(([moved[c, rows] for c in range(3)], [moved[c + 3, rows] for c in range(3)], rates[rows]))
        u = [sample(boxes_split[q], state[q][0]) for q in halves]
        mid = []
        for q in halves:
            x, v, rate = state[q]
            vm = [v[c] + (0.5 * STEP_SIZE) * (u[q][c] - v[c]) * rate for c in range(3)]
            mid.append(([x[c] + (0.5 * STEP_SIZE) * v[c] for c in range(3)], vm))
        um = [sample(boxes_split[q], mid[q][0]) for q in halves]
        for q in halves:
            rows = pl.ds(q * HALF, HALF)
            x, v, rate = state[q]
            vm = mid[q][1]
            for c in range(3):
                moved[c, rows] = x[c] + STEP_SIZE * vm[c]
                moved[c + 3, rows] = v[c] + STEP_SIZE * (um[q][c] - vm[c]) * rate
        return carry

    for _ in range(SUBSTEPS):
        substep(0, 0)
    keep = lax.broadcasted_iota(jnp.int32, (bins, part), 0) < live[0]
    for c in range(6):
        end = jnp.where(keep, moved[c], parts[c])
        moved[c] = end + 0.5 if c < 3 else end
    store = pltpu.make_async_copy(moved, out, out_sem)
    store.start()
    store.wait()


def body(velocity_field, particle_state, stokes_time, box_base, live_bins):
    n_slab, n_sub = lax.axis_size("slab"), lax.axis_size("sub")
    _, cx, cy, nz = velocity_field.shape
    tiles = nz // LANES
    bins, _, part = particle_state.shape
    hbm = pl.BlockSpec(memory_space=pltpu.HBM)
    by_row = (1, 0, 2)
    out = pl.pallas_call(
        functools.partial(kernel, n_slab, n_sub),
        out_shape=jax.ShapeDtypeStruct((6, bins, part), jnp.float32),
        in_specs=[hbm] * 4 + [pl.BlockSpec(memory_space=pltpu.SMEM)],
        out_specs=pl.BlockSpec(memory_space=pl.ANY),
        scratch_shapes=[
            pltpu.VMEM((3, cx + 2 * WIDTH, tiles, cy + 2 * TOP, LANES), jnp.float32),
            pltpu.VMEM((6, bins, part), jnp.float32),
            pltpu.VMEM((bins, part), jnp.float32),
            pltpu.VMEM((6, bins, part), jnp.float32),
            pltpu.VMEM((bins, LINES, LANES), jnp.float32),
            pltpu.VMEM((bins // HALF, LINES, LANES), jnp.float32),
            pltpu.VMEM((bins // HALF, 24 * HALF, 2 * LANES), jnp.bfloat16),
            pltpu.SMEM((3, bins), jnp.int32),
            pltpu.SemaphoreType.DMA((5 * tiles,)),
            pltpu.SemaphoreType.DMA((3,)),
            pltpu.SemaphoreType.DMA,
            pltpu.SemaphoreType.DMA((4 * tiles + 8,)),
            pltpu.SemaphoreType.DMA((4 * tiles + 8,)),
            pltpu.SemaphoreType.REGULAR((2,)),
        ],
        compiler_params=pltpu.CompilerParams(
            collective_id=0, has_side_effects=True, vmem_limit_bytes=24 << 20
        ),
        name="particles",
    )(
        *(
            pltpu.with_memory_space_constraint(a, pltpu.HBM)
            for a in (velocity_field, particle_state.transpose(by_row), stokes_time, box_base.T)
        ),
        live_bins,
    )
    return out.transpose(by_row)


def solution(mesh):
    placed = (
        P(None, "slab", "sub", None),
        P(("slab", "sub"), None, None),
        P(("slab", "sub"), None),
        P(("slab", "sub"), None),
        P(("slab", "sub")),
    )
    return jax.shard_map(
        body, mesh=mesh, in_specs=placed, out_specs=P(("slab", "sub"), None, None), check_vma=False
    )
```

```python
import functools

import jax
import jax.numpy as jnp
from jax import lax
from jax.experimental import pallas as pl
from jax.experimental.pallas import tpu as pltpu
from jax.sharding import PartitionSpec as P

SUBSTEPS = 4
STEP_SIZE = 0.2
WIDTH = 2
LANES = 128
TOP = 8
LINES = 48
HALF = 16
MESH = pl.DeviceIdType.MESH

POWERS = (
    (-1 / 16, 9 / 16, 9 / 16, -1 / 16),
    (1 / 24, -9 / 8, 9 / 8, -1 / 24),
    (1 / 4, -1 / 4, -1 / 4, 1 / 4),
    (-1 / 6, 1 / 2, -1 / 2, 1 / 6),
)


def power_matrix(shape, power, node, same):
    out = jnp.zeros(shape, jnp.float32)
    for p in range(4):
        for n in range(4):
            out = jnp.where((power == p) & (node == n) & same, POWERS[p][n], out)
    return out


def exact_dot(a, b):
    return jnp.dot(a, b, precision=lax.Precision.HIGHEST, preferred_element_type=jnp.float32)


def split(a):
    high = a.astype(jnp.bfloat16)
    return high, (a - high.astype(jnp.float32)).astype(jnp.bfloat16)


def dot(a, b):
    return jnp.dot(a, b, preferred_element_type=jnp.float32)


def sample(box, position):
    x, y, z = position
    y2, z2 = y * y, z * z
    along_z = [None, z, z2, z2 * z]
    along_y = [None, y, y2, y2 * y]
    terms = []
    for a in along_y:
        for b in along_z:
            terms.append(jnp.ones_like(x) if a is None and b is None else a if b is None else b if a is None else a * b)
    high, low = split(jnp.concatenate(terms, axis=0))
    rows = 12 * HALF
    both = dot(box, high)
    slices = both[:rows] + dot(box[:rows], low) + both[rows:]
    velocity = []
    for c in range(3):
        i = [slices[(i * 3 + c) * HALF : (i * 3 + c + 1) * HALF] for i in range(4)]
        velocity.append(((i[3] * x + i[2]) * x + i[1]) * x + i[0])
    return velocity


def kernel(n_slab, n_sub, field, states, stokes, bases_in, live, out,
           padded, parts, rates, moved, picked, planes, boxes_split, bases,
           local_sems, part_sems, out_sem, send_sems, recv_sems, here_sems):
    _, cx, cy, nz = field.shape
    tiles = nz // LANES
    _, bins, part = states.shape
    g, s = lax.axis_index("slab"), lax.axis_index("sub")

    def at(dx, dy):
        return (lax.rem(g + dx + n_slab, n_slab), lax.rem(s + dy + n_sub, n_sub))

    left, right, down, up = at(-1, 0), at(1, 0), at(0, -1), at(0, 1)
    odd = lax.rem(g, 2) == 1
    even = jnp.logical_not(odd)

    loads = []

    def load(xs, ys):
        copies = []
        for t in range(tiles):
            n = len(loads)
            copy = pltpu.make_async_copy(
                field.at[:, xs, ys, pl.ds(t * LANES, LANES)],
                padded.at[:, shifted(xs, WIDTH), t, shifted(ys, TOP), :],
                local_sems.at[n],
            )
            copy.start()
            loads.append(copy)
            copies.append(copy)
        return copies

    def shifted(rows, by):
        return pl.ds(rows.start + by, rows.size)

    x_first, x_last, x_inner = pl.ds(0, WIDTH), pl.ds(cx - WIDTH, WIDTH), pl.ds(WIDTH, cx - 2 * WIDTH)
    last_layers = load(x_last, pl.ds(0, cy))
    y_edges = load(x_inner, pl.ds(0, TOP)) + load(x_inner, pl.ds(cy - TOP, TOP))
    first_layers = load(x_first, pl.ds(0, cy))
    rest = load(x_inner, pl.ds(TOP, cy - 2 * TOP))
    small = []
    for n, (here, there) in enumerate(((states, parts), (stokes, rates), (bases_in, bases))):
        small.append(pltpu.make_async_copy(here, there, part_sems.at[n]))
        small[-1].start()

    first, second, third, last = g == 0, g == 1, g == 2, g == n_slab - 1
    barrier = pltpu.get_barrier_semaphore()

    def tell(*offsets):
        for dx, dy in offsets:
            pl.semaphore_signal(barrier, inc=1, device_id=at(dx, dy), device_id_type=MESH)

    @pl.when(jnp.logical_not(first))
    def _():
        tell((-1, 0))

    @pl.when(even)
    def _():
        tell((0, -1), (0, 1))

    @pl.when(odd & jnp.logical_not(last))
    def _():
        tell((1, 0))

    @pl.when(odd & jnp.logical_not(second))
    def _():
        tell((-1, -1), (-1, 1))

    @pl.when(second)
    def _():
        tell((1, -1), (1, 1))

    pl.semaphore_wait(barrier, jnp.where(odd, 1, jnp.where(first, 3, jnp.where(third, 8, 6))))

    @pl.when(first)
    def _():
        tell((-1, 0))

    @pl.when(even | last)
    def _():
        pl.semaphore_signal(here_sems.at[0], inc=1, device_id=right, device_id_type=MESH)

    @pl.when(third)
    def _():
        pl.semaphore_signal(here_sems.at[1], inc=1, device_id=left, device_id_type=MESH)

    copies = []

    def remote(to, source, target):
        n = len(copies)
        copy = pltpu.make_async_remote_copy(
            src_ref=source,
            dst_ref=target,
            send_sem=send_sems.at[n],
            recv_sem=recv_sems.at[n],
            device_id=to,
            device_id_type=MESH,
        )
        copies.append(copy)
        return copy

    def cells(to, xs, ys, dx, dy):
        return remote(
            to, padded.at[:, xs, :, ys, :], padded.at[:, shifted(xs, -dx * cx), :, shifted(ys, -dy * cy), :]
        )

    low, high = pl.ds(TOP, WIDTH), pl.ds(TOP + cy - WIDTH, WIDTH)
    middle = pl.ds(TOP + WIDTH, cy - 2 * WIDTH)

    def corner_cells(to, xs, dx):
        return [
            remote(
                to,
                field.at[:, xs, ys, pl.ds(t * LANES, LANES)],
                padded.at[:, shifted(xs, WIDTH - dx * cx), t, shifted(ys, TOP), :],
            )
            for ys in (pl.ds(0, WIDTH), pl.ds(cy - WIDTH, WIDTH))
            for t in range(tiles)
        ]

    from_left, from_right = corner_cells(right, x_last, 1), corner_cells(left, x_first, -1)
    across = [
        remote(
            at(1, 1),
            field.at[:, x_last, pl.ds(cy - WIDTH, WIDTH), pl.ds(t * LANES, LANES)],
            padded.at[:, pl.ds(0, WIDTH), t, pl.ds(TOP - WIDTH, WIDTH), :],
        )
        for t in range(tiles)
    ]
    layers_left = cells(right, shifted(x_last, WIDTH), middle, 1, 0)
    layers_right = cells(left, shifted(x_first, WIDTH), middle, -1, 0)
    rows_down, rows_up = cells(up, pl.ds(WIDTH, cx), high, 0, 1), cells(down, pl.ds(WIDTH, cx), low, 0, -1)

    @pl.when(last)
    def _():
        for copy in across:
            copy.start()

    for copy in from_left:
        copy.start()
    for copy in last_layers:
        copy.wait()
    layers_left.start()

    later = first | second

    @pl.when(odd & jnp.logical_not(second))
    def _():
        pl.semaphore_wait(here_sems.at[0], 1)

    @pl.when(jnp.logical_not(later))
    def _():
        for copy in from_right:
            copy.start()

    for copy in first_layers:
        copy.wait()

    @pl.when(jnp.logical_not(later))
    def _():
        layers_right.start()

    for copy in y_edges:
        copy.wait()

    @pl.when(second)
    def _():
        pl.semaphore_wait(here_sems.at[1], 1)

    rows_down.start()
    rows_up.start()

    row = lax.broadcasted_iota(jnp.int32, (LINES, LINES), 0)
    col = lax.broadcasted_iota(jnp.int32, (LINES, LINES), 1)
    along_y = power_matrix((LINES, LINES), row % 4, col % 4, row // 4 == col // 4)
    along_x = power_matrix((LINES, LINES), row // 12, col // 12, row % 12 == col % 12)
    along_xy = exact_dot(along_x, along_y)
    zr = lax.broadcasted_iota(jnp.int32, (LANES, LANES), 0)
    zc = lax.broadcasted_iota(jnp.int32, (LANES, LANES), 1)
    along_z = [
        power_matrix((LANES, LANES), zc // HALF % 4, zr % 4, zr // 4 == zc % HALF + q * HALF) for q in range(bins // HALF)
    ]

    for copy in small:
        copy.wait()
    parts[0:3] = parts[0:3] - 0.5
    rates[...] = 1.0 / rates[...]
    moved[...] = parts[...]

    @pl.when(later)
    def _():
        pl.semaphore_wait(here_sems.at[0], 1)
        for copy in from_right:
            copy.start()
        layers_right.start()

    for corners, xs in ((from_right, pl.ds(WIDTH + cx, WIDTH)), (from_left, pl.ds(0, WIDTH))):
        for copy in corners:
            copy.wait_recv()
        cells(down, xs, low, 0, -1).start()
        onward = cells(up, xs, high, 0, 1)
        if corners is from_right:
            onward.start()
            continue

        @pl.when(jnp.logical_not(first))
        def _():
            onward.start()

    for copy in rest:
        copy.wait()

    lane = lax.broadcasted_iota(jnp.int32, (4, LANES), 1)

    def pick(layers):
        for b in range(bins):
            x0, y0, z0 = bases[0, b] + WIDTH, bases[1, b] + TOP, bases[2, b]
            here = lax.shift_right_logical(z0, 7)
            after = (here + 1) & (tiles - 1)
            first = lane >= (z0 & (LANES - 1))
            for i in layers:
                for c in range(3):
                    a = padded[c, x0 + i, here, pl.ds(y0, 4), :]
                    n = padded[c, x0 + i, after, pl.ds(y0, 4), :]
                    picked[b, pl.ds((i * 3 + c) * 4, 4), :] = jnp.where(first, a, n)

    for copy in copies:
        if not any(copy is other for other in across + [onward]):
            copy.wait_send()
            if not any(copy is corner for corner in from_left + from_right):
                copy.wait_recv()

    @pl.when(last)
    def _():
        for copy in across:
            copy.wait_send()

    @pl.when(first)
    def _():
        for copy in across:
            copy.wait_recv()

    @pl.when(jnp.logical_not(first))
    def _():
        onward.wait()

    pick(range(4))

    wide = lax.broadcasted_iota(jnp.int32, (LINES, LANES), 1)
    boxes = jnp.zeros((LINES, LANES), jnp.float32)
    for b in range(bins):
        shift = (4 * b - bases[2, b]) & (LANES - 1)
        boxes = jnp.where(wide // 4 == b, pltpu.roll(picked[b], shift, 1), boxes)
    boxes = exact_dot(along_xy, boxes)
    own = lax.broadcasted_iota(jnp.int32, (HALF, LANES), 0) == lax.broadcasted_iota(jnp.int32, (HALF, LANES), 1) % HALF
    low_lane = lax.broadcasted_iota(jnp.int32, (HALF, LANES), 1) < LANES // 2
    for q in range(bins // HALF):
        planes[q] = exact_dot(boxes, along_z[q])
        for line in range(12):
            for side in range(2):
                j = 2 * side
                even = jnp.broadcast_to(planes[q, pl.ds(line * 4 + j, 1), :], (HALF, LANES))
                odd = jnp.broadcast_to(planes[q, pl.ds(line * 4 + j + 1, 1), :], (HALF, LANES))
                high, low = split(jnp.where(own, jnp.where(low_lane, even, odd), 0.0))
                lanes = pl.ds(side * LANES, LANES)
                boxes_split[q, pl.ds(line * HALF, HALF), lanes] = high
                boxes_split[q, pl.ds((line + 12) * HALF, HALF), lanes] = low

    halves = range(bins // HALF)

    def substep(_, carry):
        state = []
        for q in halves:
            rows = pl.ds(q * HALF, HALF)
            state.append(([moved[c, rows] for c in range(3)], [moved[c + 3, rows] for c in range(3)], rates[rows]))
        u = [sample(boxes_split[q], state[q][0]) for q in halves]
        mid = []
        for q in halves:
            x, v, rate = state[q]
            vm = [v[c] + (0.5 * STEP_SIZE) * (u[q][c] - v[c]) * rate for c in range(3)]
            mid.append(([x[c] + (0.5 * STEP_SIZE) * v[c] for c in range(3)], vm))
        um = [sample(boxes_split[q], mid[q][0]) for q in halves]
        for q in halves:
            rows = pl.ds(q * HALF, HALF)
            x, v, rate = state[q]
            vm = mid[q][1]
            for c in range(3):
                moved[c, rows] = x[c] + STEP_SIZE * vm[c]
                moved[c + 3, rows] = v[c] + STEP_SIZE * (um[q][c] - vm[c]) * rate
        return carry

    for _ in range(SUBSTEPS):
        substep(0, 0)
    keep = lax.broadcasted_iota(jnp.int32, (bins, part), 0) < live[0]
    for c in range(6):
        end = jnp.where(keep, moved[c], parts[c])
        moved[c] = end + 0.5 if c < 3 else end
    store = pltpu.make_async_copy(moved, out, out_sem)
    store.start()
    store.wait()


def body(velocity_field, particle_state, stokes_time, box_base, live_bins):
    n_slab, n_sub = lax.axis_size("slab"), lax.axis_size("sub")
    _, cx, cy, nz = velocity_field.shape
    tiles = nz // LANES
    bins, _, part = particle_state.shape
    hbm = pl.BlockSpec(memory_space=pltpu.HBM)
    by_row = (1, 0, 2)
    out = pl.pallas_call(
        functools.partial(kernel, n_slab, n_sub),
        out_shape=jax.ShapeDtypeStruct((6, bins, part), jnp.float32),
        in_specs=[hbm] * 4 + [pl.BlockSpec(memory_space=pltpu.SMEM)],
        out_specs=pl.BlockSpec(memory_space=pl.ANY),
        scratch_shapes=[
            pltpu.VMEM((3, cx + 2 * WIDTH, tiles, cy + 2 * TOP, LANES), jnp.float32),
            pltpu.VMEM((6, bins, part), jnp.float32),
            pltpu.VMEM((bins, part), jnp.float32),
            pltpu.VMEM((6, bins, part), jnp.float32),
            pltpu.VMEM((bins, LINES, LANES), jnp.float32),
            pltpu.VMEM((bins // HALF, LINES, LANES), jnp.float32),
            pltpu.VMEM((bins // HALF, 24 * HALF, 2 * LANES), jnp.bfloat16),
            pltpu.SMEM((3, bins), jnp.int32),
            pltpu.SemaphoreType.DMA((5 * tiles,)),
            pltpu.SemaphoreType.DMA((3,)),
            pltpu.SemaphoreType.DMA,
            pltpu.SemaphoreType.DMA((5 * tiles + 8,)),
            pltpu.SemaphoreType.DMA((5 * tiles + 8,)),
            pltpu.SemaphoreType.REGULAR((2,)),
        ],
        compiler_params=pltpu.CompilerParams(
            collective_id=0, has_side_effects=True, vmem_limit_bytes=24 << 20
        ),
        name="particles",
    )(
        *(
            pltpu.with_memory_space_constraint(a, pltpu.HBM)
            for a in (velocity_field, particle_state.transpose(by_row), stokes_time, box_base.T)
        ),
        live_bins,
    )
    return out.transpose(by_row)


def solution(mesh):
    placed = (
        P(None, "slab", "sub", None),
        P(("slab", "sub"), None, None),
        P(("slab", "sub"), None),
        P(("slab", "sub"), None),
        P(("slab", "sub")),
    )
    return jax.shard_map(
        body, mesh=mesh, in_specs=placed, out_specs=P(("slab", "sub"), None, None), check_vma=False
    )
```

```python
import functools

import jax
import jax.numpy as jnp
from jax import lax
from jax.experimental import pallas as pl
from jax.experimental.pallas import tpu as pltpu
from jax.sharding import PartitionSpec as P

SUBSTEPS = 4
STEP_SIZE = 0.2
WIDTH = 2
LANES = 128
TOP = 8
LINES = 48
HALF = 16
MESH = pl.DeviceIdType.MESH

POWERS = (
    (-1 / 16, 9 / 16, 9 / 16, -1 / 16),
    (1 / 24, -9 / 8, 9 / 8, -1 / 24),
    (1 / 4, -1 / 4, -1 / 4, 1 / 4),
    (-1 / 6, 1 / 2, -1 / 2, 1 / 6),
)


def power_matrix(shape, power, node, same):
    out = jnp.zeros(shape, jnp.float32)
    for p in range(4):
        for n in range(4):
            out = jnp.where((power == p) & (node == n) & same, POWERS[p][n], out)
    return out


def exact_dot(a, b):
    return jnp.dot(a, b, precision=lax.Precision.HIGHEST, preferred_element_type=jnp.float32)


def split(a):
    high = a.astype(jnp.bfloat16)
    return high, (a - high.astype(jnp.float32)).astype(jnp.bfloat16)


def dot(a, b):
    return jnp.dot(a, b, preferred_element_type=jnp.float32)


def sample(box, position):
    x, y, z = position
    y2, z2 = y * y, z * z
    along_z = [None, z, z2, z2 * z]
    along_y = [None, y, y2, y2 * y]
    terms = []
    for a in along_y:
        for b in along_z:
            terms.append(jnp.ones_like(x) if a is None and b is None else a if b is None else b if a is None else a * b)
    high, low = split(jnp.concatenate(terms, axis=0))
    rows = 12 * HALF
    both = dot(box, high)
    slices = both[:rows] + dot(box[:rows], low) + both[rows:]
    velocity = []
    for c in range(3):
        i = [slices[(i * 3 + c) * HALF : (i * 3 + c + 1) * HALF] for i in range(4)]
        velocity.append(((i[3] * x + i[2]) * x + i[1]) * x + i[0])
    return velocity


def kernel(n_slab, n_sub, field, states, stokes, bases_in, live, out,
           padded, parts, rates, moved, picked, planes, boxes_split, bases,
           local_sems, part_sems, out_sem, send_sems, recv_sems, here_sems):
    _, cx, cy, nz = field.shape
    tiles = nz // LANES
    _, bins, part = states.shape
    g, s = lax.axis_index("slab"), lax.axis_index("sub")

    def at(dx, dy):
        return (lax.rem(g + dx + n_slab, n_slab), lax.rem(s + dy + n_sub, n_sub))

    left, right, down, up = at(-1, 0), at(1, 0), at(0, -1), at(0, 1)
    odd = lax.rem(g, 2) == 1
    even = jnp.logical_not(odd)

    loads = []

    def load(xs, ys):
        copies = []
        for t in range(tiles):
            n = len(loads)
            copy = pltpu.make_async_copy(
                field.at[:, xs, ys, pl.ds(t * LANES, LANES)],
                padded.at[:, shifted(xs, WIDTH), t, shifted(ys, TOP), :],
                local_sems.at[n],
            )
            copy.start()
            loads.append(copy)
            copies.append(copy)
        return copies

    def shifted(rows, by):
        return pl.ds(rows.start + by, rows.size)

    x_first, x_last, x_inner = pl.ds(0, WIDTH), pl.ds(cx - WIDTH, WIDTH), pl.ds(WIDTH, cx - 2 * WIDTH)
    last_layers = load(x_last, pl.ds(0, cy))
    y_edges = load(x_inner, pl.ds(0, TOP)) + load(x_inner, pl.ds(cy - TOP, TOP))
    first_layers = load(x_first, pl.ds(0, cy))
    rest = load(x_inner, pl.ds(TOP, cy - 2 * TOP))
    small = []
    for n, (here, there) in enumerate(((states, parts), (stokes, rates), (bases_in, bases))):
        small.append(pltpu.make_async_copy(here, there, part_sems.at[n]))
        small[-1].start()

    first, second, third, last = g == 0, g == 1, g == 2, g == n_slab - 1
    barrier = pltpu.get_barrier_semaphore()

    def tell(*offsets):
        for dx, dy in offsets:
            pl.semaphore_signal(barrier, inc=1, device_id=at(dx, dy), device_id_type=MESH)

    @pl.when(jnp.logical_not(first))
    def _():
        tell((-1, 0))

    @pl.when(even)
    def _():
        tell((0, -1), (0, 1))

    @pl.when(odd & jnp.logical_not(last))
    def _():
        tell((1, 0))

    @pl.when(odd & jnp.logical_not(second))
    def _():
        tell((-1, -1), (-1, 1))

    @pl.when(second)
    def _():
        tell((1, -1), (1, 1))

    pl.semaphore_wait(barrier, jnp.where(odd, 1, jnp.where(first, 3, jnp.where(third, 8, 6))))

    @pl.when(first)
    def _():
        tell((-1, 0))

    @pl.when(even | last)
    def _():
        pl.semaphore_signal(here_sems.at[0], inc=1, device_id=right, device_id_type=MESH)

    @pl.when(third)
    def _():
        pl.semaphore_signal(here_sems.at[1], inc=1, device_id=left, device_id_type=MESH)

    copies = []

    def remote(to, source, target):
        n = len(copies)
        copy = pltpu.make_async_remote_copy(
            src_ref=source,
            dst_ref=target,
            send_sem=send_sems.at[n],
            recv_sem=recv_sems.at[n],
            device_id=to,
            device_id_type=MESH,
        )
        copies.append(copy)
        return copy

    def cells(to, xs, ys, dx, dy):
        return remote(
            to, padded.at[:, xs, :, ys, :], padded.at[:, shifted(xs, -dx * cx), :, shifted(ys, -dy * cy), :]
        )

    low, high = pl.ds(TOP, WIDTH), pl.ds(TOP + cy - WIDTH, WIDTH)
    middle = pl.ds(TOP + WIDTH, cy - 2 * WIDTH)

    def corner_cells(to, xs, dx):
        return [
            remote(
                to,
                field.at[:, xs, ys, pl.ds(t * LANES, LANES)],
                padded.at[:, shifted(xs, WIDTH - dx * cx), t, shifted(ys, TOP), :],
            )
            for ys in (pl.ds(0, WIDTH), pl.ds(cy - WIDTH, WIDTH))
            for t in range(tiles)
        ]

    from_left, from_right = corner_cells(right, x_last, 1), corner_cells(left, x_first, -1)
    across = [
        remote(
            at(1, 1),
            field.at[:, x_last, pl.ds(cy - WIDTH, WIDTH), pl.ds(t * LANES, LANES)],
            padded.at[:, pl.ds(0, WIDTH), t, pl.ds(TOP - WIDTH, WIDTH), :],
        )
        for t in range(tiles)
    ]
    layers_left = cells(right, shifted(x_last, WIDTH), middle, 1, 0)
    layers_right = cells(left, shifted(x_first, WIDTH), middle, -1, 0)
    rows_down, rows_up = (
        [cells(to, pl.ds(x, n), rows, 0, dy) for x, n in ((2 * WIDTH, cx - WIDTH), (WIDTH, WIDTH))]
        for to, rows, dy in ((up, high, 1), (down, low, -1))
    )

    @pl.when(last)
    def _():
        for copy in across:
            copy.start()

    for copy in from_left:
        copy.start()
    for copy in last_layers:
        copy.wait()
    layers_left.start()

    later = first | second

    @pl.when(odd & jnp.logical_not(second))
    def _():
        pl.semaphore_wait(here_sems.at[0], 1)

    @pl.when(jnp.logical_not(later))
    def _():
        for copy in from_right:
            copy.start()

    for copy in y_edges:
        copy.wait()

    @pl.when(second)
    def _():
        pl.semaphore_wait(here_sems.at[1], 1)

    rows_down[0].start()
    rows_up[0].start()
    for copy in first_layers:
        copy.wait()
    rows_down[1].start()
    rows_up[1].start()

    @pl.when(jnp.logical_not(later))
    def _():
        layers_right.start()

    row = lax.broadcasted_iota(jnp.int32, (LINES, LINES), 0)
    col = lax.broadcasted_iota(jnp.int32, (LINES, LINES), 1)
    along_y = power_matrix((LINES, LINES), row % 4, col % 4, row // 4 == col // 4)
    along_x = power_matrix((LINES, LINES), row // 12, col // 12, row % 12 == col % 12)
    along_xy = exact_dot(along_x, along_y)
    zr = lax.broadcasted_iota(jnp.int32, (LANES, LANES), 0)
    zc = lax.broadcasted_iota(jnp.int32, (LANES, LANES), 1)
    along_z = [
        power_matrix((LANES, LANES), zc // HALF % 4, zr % 4, zr // 4 == zc % HALF + q * HALF) for q in range(bins // HALF)
    ]

    for copy in small:
        copy.wait()
    parts[0:3] = parts[0:3] - 0.5
    rates[...] = 1.0 / rates[...]
    moved[...] = parts[...]

    @pl.when(later)
    def _():
        pl.semaphore_wait(here_sems.at[0], 1)
        for copy in from_right:
            copy.start()
        layers_right.start()

    for corners, xs in ((from_right, pl.ds(WIDTH + cx, WIDTH)), (from_left, pl.ds(0, WIDTH))):
        for copy in corners:
            copy.wait_recv()
        cells(down, xs, low, 0, -1).start()
        onward = cells(up, xs, high, 0, 1)
        if corners is from_right:
            onward.start()
            continue

        @pl.when(jnp.logical_not(first))
        def _():
            onward.start()

    for copy in rest:
        copy.wait()

    lane = lax.broadcasted_iota(jnp.int32, (4, LANES), 1)

    def pick(layers):
        for b in range(bins):
            x0, y0, z0 = bases[0, b] + WIDTH, bases[1, b] + TOP, bases[2, b]
            here = lax.shift_right_logical(z0, 7)
            after = (here + 1) & (tiles - 1)
            first = lane >= (z0 & (LANES - 1))
            for i in layers:
                for c in range(3):
                    a = padded[c, x0 + i, here, pl.ds(y0, 4), :]
                    n = padded[c, x0 + i, after, pl.ds(y0, 4), :]
                    picked[b, pl.ds((i * 3 + c) * 4, 4), :] = jnp.where(first, a, n)

    for copy in copies:
        if not any(copy is other for other in across + [onward]):
            copy.wait_send()
            if not any(copy is corner for corner in from_left + from_right):
                copy.wait_recv()

    @pl.when(last)
    def _():
        for copy in across:
            copy.wait_send()

    @pl.when(first)
    def _():
        for copy in across:
            copy.wait_recv()

    @pl.when(jnp.logical_not(first))
    def _():
        onward.wait()

    pick(range(4))

    wide = lax.broadcasted_iota(jnp.int32, (LINES, LANES), 1)
    boxes = jnp.zeros((LINES, LANES), jnp.float32)
    for b in range(bins):
        shift = (4 * b - bases[2, b]) & (LANES - 1)
        boxes = jnp.where(wide // 4 == b, pltpu.roll(picked[b], shift, 1), boxes)
    boxes = exact_dot(along_xy, boxes)
    own = lax.broadcasted_iota(jnp.int32, (HALF, LANES), 0) == lax.broadcasted_iota(jnp.int32, (HALF, LANES), 1) % HALF
    low_lane = lax.broadcasted_iota(jnp.int32, (HALF, LANES), 1) < LANES // 2
    for q in range(bins // HALF):
        planes[q] = exact_dot(boxes, along_z[q])
        for line in range(12):
            for side in range(2):
                j = 2 * side
                even = jnp.broadcast_to(planes[q, pl.ds(line * 4 + j, 1), :], (HALF, LANES))
                odd = jnp.broadcast_to(planes[q, pl.ds(line * 4 + j + 1, 1), :], (HALF, LANES))
                high, low = split(jnp.where(own, jnp.where(low_lane, even, odd), 0.0))
                lanes = pl.ds(side * LANES, LANES)
                boxes_split[q, pl.ds(line * HALF, HALF), lanes] = high
                boxes_split[q, pl.ds((line + 12) * HALF, HALF), lanes] = low

    halves = range(bins // HALF)

    def substep(_, carry):
        state = []
        for q in halves:
            rows = pl.ds(q * HALF, HALF)
            state.append(([moved[c, rows] for c in range(3)], [moved[c + 3, rows] for c in range(3)], rates[rows]))
        u = [sample(boxes_split[q], state[q][0]) for q in halves]
        mid = []
        for q in halves:
            x, v, rate = state[q]
            vm = [v[c] + (0.5 * STEP_SIZE) * (u[q][c] - v[c]) * rate for c in range(3)]
            mid.append(([x[c] + (0.5 * STEP_SIZE) * v[c] for c in range(3)], vm))
        um = [sample(boxes_split[q], mid[q][0]) for q in halves]
        for q in halves:
            rows = pl.ds(q * HALF, HALF)
            x, v, rate = state[q]
            vm = mid[q][1]
            for c in range(3):
                moved[c, rows] = x[c] + STEP_SIZE * vm[c]
                moved[c + 3, rows] = v[c] + STEP_SIZE * (um[q][c] - vm[c]) * rate
        return carry

    for _ in range(SUBSTEPS):
        substep(0, 0)
    keep = lax.broadcasted_iota(jnp.int32, (bins, part), 0) < live[0]
    for c in range(6):
        end = jnp.where(keep, moved[c], parts[c])
        moved[c] = end + 0.5 if c < 3 else end
    store = pltpu.make_async_copy(moved, out, out_sem)
    store.start()
    store.wait()


def body(velocity_field, particle_state, stokes_time, box_base, live_bins):
    n_slab, n_sub = lax.axis_size("slab"), lax.axis_size("sub")
    _, cx, cy, nz = velocity_field.shape
    tiles = nz // LANES
    bins, _, part = particle_state.shape
    hbm = pl.BlockSpec(memory_space=pltpu.HBM)
    by_row = (1, 0, 2)
    out = pl.pallas_call(
        functools.partial(kernel, n_slab, n_sub),
        out_shape=jax.ShapeDtypeStruct((6, bins, part), jnp.float32),
        in_specs=[hbm] * 4 + [pl.BlockSpec(memory_space=pltpu.SMEM)],
        out_specs=pl.BlockSpec(memory_space=pl.ANY),
        scratch_shapes=[
            pltpu.VMEM((3, cx + 2 * WIDTH, tiles, cy + 2 * TOP, LANES), jnp.float32),
            pltpu.VMEM((6, bins, part), jnp.float32),
            pltpu.VMEM((bins, part), jnp.float32),
            pltpu.VMEM((6, bins, part), jnp.float32),
            pltpu.VMEM((bins, LINES, LANES), jnp.float32),
            pltpu.VMEM((bins // HALF, LINES, LANES), jnp.float32),
            pltpu.VMEM((bins // HALF, 24 * HALF, 2 * LANES), jnp.bfloat16),
            pltpu.SMEM((3, bins), jnp.int32),
            pltpu.SemaphoreType.DMA((5 * tiles,)),
            pltpu.SemaphoreType.DMA((3,)),
            pltpu.SemaphoreType.DMA,
            pltpu.SemaphoreType.DMA((5 * tiles + 10,)),
            pltpu.SemaphoreType.DMA((5 * tiles + 10,)),
            pltpu.SemaphoreType.REGULAR((2,)),
        ],
        compiler_params=pltpu.CompilerParams(
            collective_id=0, has_side_effects=True, vmem_limit_bytes=24 << 20
        ),
        name="particles",
    )(
        *(
            pltpu.with_memory_space_constraint(a, pltpu.HBM)
            for a in (velocity_field, particle_state.transpose(by_row), stokes_time, box_base.T)
        ),
        live_bins,
    )
    return out.transpose(by_row)


def solution(mesh):
    placed = (
        P(None, "slab", "sub", None),
        P(("slab", "sub"), None, None),
        P(("slab", "sub"), None),
        P(("slab", "sub"), None),
        P(("slab", "sub")),
    )
    return jax.shard_map(
        body, mesh=mesh, in_specs=placed, out_specs=P(("slab", "sub"), None, None), check_vma=False
    )
```
